1024 devices in a mesh: seq: 64 (over z, x), head: 16 (over y, core).
Axes of the slice: x: 4, y: 8, z: 16, core: 2. Of those that a mesh axis runs over, the one named last changes fastest.
Arguments:
- query_rows: bfloat16 [65536, 16, 128], P('seq', 'head'), may hold values from -130 to 130
- key_rows: bfloat16 [65536, 16, 128], P('seq', 'head'), may hold values from -0.52734375 to 0.52734375
- value_rows: bfloat16 [65536, 16, 128], P('seq', 'head'), may hold values from -6 to 6
- log_gate: float32 [16, 65536], P('head', 'seq'), may hold values from -1 to 0
- norm_gain: float32 [16, 128], P('head'), may hold values from 0.5 to 1.5
- doc_ends: int32 [4096], P('seq'), may hold values from 0 to 1024, as said below
- doc_page: int32 [4096], replicated, may hold values from -1 to 4095, as said below
Outputs:
- attended: bfloat16 [65536, 16, 128], P('seq', 'head')
- state_cache: bfloat16 [4096, 16, 128, 128], P('seq', 'head')
The draws below stay inside these ranges and needn't reach their ends.
Inputs may be any that keep to these rules, and one draw needn't show every extreme that they name: `doc_ends`: index s of seq holds entries s * 64 to s * 64 + 63: its nonzero entries come first and rise strictly. An entry e means that a document ends after local token e - 1 and, if e < 1024, a new one starts at local token e; zeros are unused. Some index of seq uses all 64 entries and some index uses none. `doc_page`: entry i is the cache page, owned by index page // 64 of seq, that receives the state of the document ended by doc_ends entry i, and -1 exactly where that entry is 0. No page is named twice, and the documents ending on one index of seq go to different owners.
All inputs are finite; a program needn't handle non-finite values.
Results may differ from the reference program's by a relative error of at most 0.0044.
Values may be sent and summed in bfloat16 or wider, within the bound.
A program may use at most 32 MiB of HBM per device.

```python
import math
import jax
import jax.numpy as jnp
from jax import lax

HEADS = 16
DK = 128
DV = 128
TOK_DEV = 1024
SPAN = 512
BOUNDS = 64
PAGES_DEV = 64
TOKENS = 65536
PAGES = 4096


def doc_layout(key):
    base = jax.random.fold_in(key, 101)
    subkeys = jax.random.split(base, 8)
    devices = TOKENS // TOK_DEV
    indices = jnp.arange(devices, dtype=jnp.int32)
    columns = jnp.arange(BOUNDS, dtype=jnp.int32)
    span_length = max(devices // 4, 1)
    run_start = jax.random.randint(subkeys[0], (), 0, devices - span_length + 1)
    in_run = (indices >= run_start) & (indices < run_start + span_length)
    outside_pick = jax.random.randint(subkeys[1], (), 0, devices - span_length)
    full_device = jnp.where(outside_pick < run_start, outside_pick, outside_pick + span_length)
    counts = jax.random.randint(subkeys[3], (devices,), BOUNDS // 4, BOUNDS + 1)
    counts = jnp.where(indices == full_device, BOUNDS, counts)
    counts = jnp.where(in_run, 0, counts)
    device_keys = jax.random.split(subkeys[4], devices)

    def pick_offsets(single_key, count_here):
        chosen = jax.random.permutation(single_key, TOK_DEV - 1)[:BOUNDS] + 1
        chosen = jnp.where(columns < count_here, chosen, TOK_DEV + 1)
        return jnp.sort(chosen)
    picked = jax.vmap(pick_offsets)(device_keys, counts)
    picked = jnp.where((indices == full_device)[:, None] & (columns == BOUNDS - 1)[None, :], TOK_DEV, picked)
    active = columns[None, :] < counts[:, None]
    ends = jnp.where(active, picked, 0)
    offsets = 1 + columns
    sigma = jax.random.permutation(subkeys[6], devices)
    inverse = jnp.argsort(sigma)
    target_pos = (inverse[full_device] + offsets[0]) % devices
    displaced = sigma[target_pos]
    sigma = jnp.where(sigma == devices - 1, displaced, jnp.where(indices == target_pos, devices - 1, sigma))
    inverse = jnp.argsort(sigma)
    owners = sigma[(inverse[:, None] + offsets[None, :]) % devices]
    page_keys = jax.random.split(subkeys[7], devices)

    def page_order(single_key):
        return jax.random.permutation(single_key, PAGES_DEV)
    orders = jax.vmap(page_order)(page_keys)
    last_row = (orders[devices - 1] + PAGES_DEV - 1 - orders[devices - 1, 0]) % PAGES_DEV
    orders = orders.at[devices - 1].set(last_row)
    local_page = orders[owners, columns[None, :]]
    pages = jnp.where(active, owners * PAGES_DEV + local_page, -1)
    return (ends.reshape(-1).astype(jnp.int32), pages.reshape(-1).astype(jnp.int32))


def draw_doc_ends(key, part):
    return doc_layout(key)[0]


def draw_doc_page(key, part):
    return doc_layout(key)[1]


def draw_query_rows(key, part):
    subkeys = jax.random.split(key, 1)
    ramp = jnp.arange(HEADS, dtype=jnp.float32) / (HEADS - 1)
    values = jnp.clip(jax.random.normal(subkeys[0], (TOKENS, HEADS, DK)), -6.0, 6.0)
    values = values * (3.0 ** ramp)[None, :, None]
    return values.astype(jnp.float32).astype(jnp.bfloat16)


def draw_log_gate(key, part):
    subkeys = jax.random.split(key, 7)
    devices = TOKENS // TOK_DEV
    share = 0.5
    rough_low = 0.5
    rough_high = 1.5
    fast = jax.random.uniform(subkeys[0], (HEADS,)) < share
    quick = 1.0 / 40.0 * jnp.exp(jax.random.uniform(subkeys[1], (HEADS,), minval=math.log(0.6), maxval=math.log(1.6)))
    slow = math.log(10.0) / TOKENS * jnp.exp(jax.random.uniform(subkeys[2], (HEADS,), minval=math.log(0.02), maxval=math.log(0.1)))
    base_rate = jnp.where(fast, quick, slow)
    device_factor = jnp.exp(jax.random.uniform(subkeys[3], (HEADS, devices), minval=math.log(0.5), maxval=math.log(2.0)))
    device_factor = jnp.repeat(device_factor, TOK_DEV, axis=1)
    rough = jax.random.uniform(subkeys[4], (HEADS, TOKENS), minval=rough_low, maxval=rough_high)
    gate_values = -base_rate[:, None] * device_factor * rough
    slot_positions = jax.random.randint(subkeys[5], (2,), 0, TOKENS)
    gate_strength = jax.random.uniform(subkeys[6], (2, HEADS), minval=0.5, maxval=0.8)
    state_slots = jnp.arange(TOKENS, dtype=jnp.int32)
    for run_group_index in range(2):
        gate_values = gate_values + jnp.where(state_slots[None, :] == slot_positions[run_group_index], jnp.log(gate_strength[run_group_index])[:, None], 0.0)
    return gate_values.astype(jnp.float32)


def level_of(stream_key, shape, cuts, smallest, largest):
    def one(position, blocks):
        steps = jax.random.uniform(jax.random.fold_in(jax.random.fold_in(stream_key, 6), position), (blocks,), jnp.float32, smallest / len(cuts), largest / len(cuts))
        return jnp.repeat(jnp.exp(steps), shape[position] // blocks).reshape((-1,) + (1,) * (len(shape) - position - 1))

    loudness = one(*cuts[0])
    for cut in cuts[1:]:
        loudness = loudness * one(*cut)
    return loudness


def scatter_about(stream_key, dims, deviation, reach, cuts=(), kind=jnp.bfloat16):
    factor_of = level_of(stream_key, dims, cuts, -0.22, 0.18) if cuts else 1.0
    array = jax.random.normal(stream_key, dims, jnp.float32) * deviation * factor_of
    return jnp.minimum(jnp.maximum(array, -reach), reach).astype(kind)


def setup_inputs(seed: int = 0) -> dict:
    seeds = jax.random.split(jax.random.key(seed), 8)
    return {
        "query_rows": draw_query_rows(jax.random.fold_in(seeds[7], 71), 0),
        "key_rows": scatter_about(seeds[1], (TOKENS, HEADS, DK), (DK ** -0.5), 0.52734375, ((0, 64), (1, 16))),
        "value_rows": scatter_about(seeds[2], (TOKENS, HEADS, DV), 1.0, 6.0, ((0, 64), (1, 16))),
        "log_gate": draw_log_gate(jax.random.fold_in(seeds[7], 71), 0),
        "norm_gain": jnp.clip(1.0 + 0.1 * jax.random.normal(seeds[4], (HEADS, DV), jnp.float32), 0.5, 1.5),
        "doc_ends": draw_doc_ends(jax.random.fold_in(seeds[7], 71), 0),
        "doc_page": draw_doc_page(jax.random.fold_in(seeds[7], 71), 0),
    }


epsilon = 1e-05
precise = lax.Precision.HIGHEST

def block_weights(query_block, key_block, running_total, segment_block):
    length = segment_block.shape[0]
    slot_positions = jnp.arange(length, dtype=jnp.int32)
    allowed = (slot_positions[:, None] >= slot_positions[None, :]) & (segment_block[:, None] == segment_block[None, :])
    spread = running_total[:, :, None] - running_total[:, None, :]
    damping = jnp.exp(jnp.where(allowed[None], spread, -jnp.inf))
    scores = jnp.einsum('thd,shd->hts', query_block.astype(jnp.float32), key_block.astype(jnp.float32))
    return (scores * damping).astype(jnp.bfloat16)

def row_weights(running_total, segment_block, seg_before, row_index):
    length = segment_block.shape[0]
    slot_positions = jnp.arange(length, dtype=jnp.int32)
    segment_row = segment_block[row_index]
    row_level = running_total[:, row_index]
    allowed = (slot_positions <= row_index) & (segment_block == segment_row)
    weights = jnp.exp(jnp.where(allowed[None, :], row_level[:, None] - running_total, -jnp.inf))
    carry_keep = jnp.where(segment_row == seg_before, jnp.exp(row_level), 0.0)
    return (weights, carry_keep)

def row_state(entry_state, key_block, value_block, running_total, segment_block, seg_before, row_index):
    weights, carry_keep = row_weights(running_total, segment_block, seg_before, row_index)
    scaled = key_block.astype(jnp.float32) * weights.T[:, :, None]
    fresh = jnp.einsum('shd,shv->hdv', scaled, value_block.astype(jnp.float32), precision=precise)
    return carry_keep[:, None, None] * entry_state + fresh

def end_state(entry_state, key_block, value_block, running_total, segment_block, seg_before, row_index):
    weights, carry_keep = row_weights(running_total, segment_block, seg_before, row_index)
    decayed = (key_block.astype(jnp.float32) * weights.T[:, :, None]).astype(jnp.bfloat16)
    fresh = jnp.einsum('shd,shv->hdv', decayed.astype(jnp.float32), value_block.astype(jnp.float32), precision=precise)
    return carry_keep[:, None, None] * entry_state + fresh

def block_step(carry_in, inputs):
    state_in, seg_before = carry_in
    query_block, key_block, value_block, gate_block, segment_block = inputs
    running_total = jnp.cumsum(gate_block, axis=1)
    weights = block_weights(query_block, key_block, running_total, segment_block)
    within_block = jnp.einsum('hts,shv->thv', weights.astype(jnp.float32), value_block.astype(jnp.float32))
    carry_reach = jnp.where((segment_block == seg_before)[None, :], jnp.exp(running_total), 0.0)
    from_before = jnp.einsum('thd,hdv->thv', query_block.astype(jnp.float32), state_in, precision=precise) * carry_reach.T[:, :, None]
    new_state = row_state(state_in, key_block, value_block, running_total, segment_block, seg_before, segment_block.shape[0] - 1)
    return ((new_state, segment_block[-1]), (within_block + from_before, state_in))

def reference(query_rows, key_rows, value_rows, log_gate, norm_gain, doc_ends, doc_page):
    devices = TOKENS // TOK_DEV
    blocks = TOKENS // SPAN
    end_table = doc_ends.reshape(devices, BOUNDS)
    anchors = (jnp.arange(devices, dtype=jnp.int32) * TOK_DEV)[:, None]
    starts = jnp.where(end_table > 0, anchors + end_table, TOKENS).reshape(-1).astype(jnp.int32)
    start_marks = jnp.zeros((TOKENS + 1,), jnp.int32).at[starts].add(1)
    segment = jnp.cumsum(start_marks[:TOKENS]).astype(jnp.int32)
    inputs = (query_rows.reshape(blocks, SPAN, HEADS, DK), key_rows.reshape(blocks, SPAN, HEADS, DK), value_rows.reshape(blocks, SPAN, HEADS, DV), log_gate.reshape(HEADS, blocks, SPAN).transpose(1, 0, 2), segment.reshape(blocks, SPAN))
    initial = (jnp.zeros((HEADS, DK, DV), jnp.float32), jnp.zeros((), jnp.int32))
    final_carry, (mixed_out, entries) = lax.scan(block_step, initial, inputs)
    mixed_out = mixed_out.reshape(TOKENS, HEADS, DV)
    mean_square = lax.optimization_barrier(jnp.mean(mixed_out * mixed_out, axis=(1, 2)))
    attended = (mixed_out * lax.rsqrt(mean_square + epsilon)[:, None, None] * norm_gain[None]).astype(jnp.bfloat16)
    seg_before_all = jnp.concatenate([jnp.zeros((1,), jnp.int32), segment.reshape(blocks, SPAN)[:-1, -1]])

    def finish(slot_index):
        device = slot_index // BOUNDS
        ending = doc_ends[slot_index]
        row_global = (device * TOK_DEV + jnp.maximum(ending, 1) - 1).astype(jnp.int32)
        block_index = row_global // SPAN
        first_row = (block_index * SPAN).astype(jnp.int32)
        key_block = lax.dynamic_slice_in_dim(key_rows, first_row, SPAN, 0)
        value_block = lax.dynamic_slice_in_dim(value_rows, first_row, SPAN, 0)
        gate_block = lax.dynamic_slice_in_dim(log_gate, first_row, SPAN, 1)
        segment_block = lax.dynamic_slice_in_dim(segment, first_row, SPAN, 0)
        state_end = end_state(entries[block_index], key_block, value_block, jnp.cumsum(gate_block, axis=1), segment_block, seg_before_all[block_index], row_global - first_row)
        return state_end.astype(jnp.bfloat16)
    finished = lax.map(finish, jnp.arange(devices * BOUNDS, dtype=jnp.int32))
    targets = jnp.where(doc_page >= 0, doc_page, PAGES).astype(jnp.int32)
    state_cache = jnp.zeros((PAGES, HEADS, DK, DV), jnp.bfloat16).at[targets].set(finished, mode='drop')
    return (attended, state_cache)
```

```python
import functools

import jax
import jax.numpy as jnp
from jax import lax
from jax.experimental import pallas as pl
from jax.experimental.pallas import tpu as pltpu
from jax.sharding import PartitionSpec as P

EPS = 1e-05
RING = 4
TILE = 128
MESH = pl.DeviceIdType.MESH
F32 = jnp.float32
BF16 = jnp.bfloat16


def row_to_col(row):
    n = row.shape[1]
    eye = lax.broadcasted_iota(jnp.int32, (n, n), 0) == lax.broadcasted_iota(jnp.int32, (n, n), 1)
    return jnp.sum(jnp.where(eye, jnp.broadcast_to(row, (n, n)), 0.0), axis=1, keepdims=True)


def spread_col(row):
    n = row.shape[1]
    return jnp.transpose(jnp.broadcast_to(row, (n, n)))


def running_sum(gates):
    rows, lanes = gates.shape
    lane = lax.broadcasted_iota(jnp.int32, gates.shape, 1)
    sub = lax.broadcasted_iota(jnp.int32, gates.shape, 0)
    total = gates
    step = 1
    while step < lanes:
        total = total + jnp.where(lane >= step, pltpu.roll(total, step, 1), 0.0)
        step *= 2
    last = jnp.broadcast_to(total[:, lanes - 1 :], gates.shape)
    before = jnp.where(sub >= 1, pltpu.roll(last, 1, 0), 0.0)
    step = 1
    while step < rows:
        before = before + jnp.where(sub >= step, pltpu.roll(before, step, 0), 0.0)
        step *= 2
    return total + before


def front(
    groups,
    q_ref,
    k_ref,
    v_ref,
    gate_ref,
    ends_ref,
    page_ref,
    slots_ref,
    mixed_ref,
    squares_ref,
    raw_t,
    scaled_t,
    lhs,
    state,
    link,
    x_state,
    x_link,
    z_out,
    z_link_out,
    z_state,
    z_link,
    back_out,
    back_in,
    first_state,
    sem_xs,
    sem_xr,
    sem_xls,
    sem_xlr,
    sem_zs,
    sem_zr,
    sem_zls,
    sem_zlr,
    sem_bs,
    sem_br,
):
    place = lax.axis_index("seq")
    head = lax.axis_index("head")
    z, x = place // RING, place % RING
    tokens, depth = k_ref.shape
    tiles = tokens // TILE
    docs = ends_ref.shape[1]
    owners = slots_ref.shape[0]
    quarter = depth // RING

    barrier = pltpu.get_barrier_semaphore()
    for hop in range(1, RING):
        peer = z * RING + (x + hop) % RING
        pl.semaphore_signal(barrier, inc=1, device_id=(peer, head), device_id_type=MESH)
    for hop in range(1, groups):
        peer = ((z + hop) % groups) * RING + x
        pl.semaphore_signal(barrier, inc=1, device_id=(peer, head), device_id_type=MESH)

    cum = running_sum(gate_ref[...])
    ends = row_to_col(ends_ref[...].astype(F32))
    pages = page_ref[pl.ds(place, 1), :]
    owner = row_to_col((pages >> (owners.bit_length() - 1)).astype(F32))
    used = ends > 0.0
    lane = lax.broadcasted_iota(jnp.int32, (docs, TILE), 1).astype(F32)
    doc = lax.broadcasted_iota(jnp.int32, (docs, TILE), 0).astype(F32)
    cum_row = [cum[t : t + 1, :] for t in range(tiles)]
    total = cum[tiles - 1 :, TILE - 1 :]
    seg_row = []
    at_end = jnp.zeros((docs, 1), F32)
    for t in range(tiles):
        position = lane + float(t * TILE)
        seg_row.append(
            jnp.sum(jnp.where(used & (ends <= position), 1.0, 0.0), axis=0, keepdims=True)
        )
        at_end = at_end + jnp.sum(
            jnp.where(position == ends - 1.0, jnp.broadcast_to(cum_row[t], position.shape), 0.0),
            axis=1,
            keepdims=True,
        )
    own_row, open_row = [], []
    for t in range(tiles):
        inside = (jnp.broadcast_to(seg_row[t], doc.shape) == doc) & used
        done = jnp.sum(jnp.where(inside, 1.0, 0.0), axis=0, keepdims=True)
        stop = jnp.sum(jnp.where(inside, at_end, 0.0), axis=0, keepdims=True)
        owned = jnp.sum(jnp.where(inside, owner, 0.0), axis=0, keepdims=True)
        stop = jnp.where(done > 0.0, stop, total)
        own_row.append(jnp.where(done > 0.0, owned, -1.0))
        open_row.append(jnp.where(done > 0.0, 0.0, 1.0))
        weight = jnp.exp(stop - cum_row[t])
        turned = jnp.transpose(k_ref[pl.ds(t * TILE, TILE), :].astype(F32))
        cols = pl.ds(t * TILE, TILE)
        raw_t[:, cols] = turned.astype(BF16)
        turned = turned * weight
        high = turned.astype(BF16)
        scaled_t[:, cols] = high
        keep = open_row[t]
        low = ((turned - high.astype(F32)) * keep).astype(BF16)
        values = v_ref[pl.ds(t * TILE, TILE), :]
        piece = jnp.dot((high.astype(F32) * keep).astype(BF16), values, preferred_element_type=F32)
        piece = piece + jnp.dot(low, values, preferred_element_type=F32)
        if t == 0:
            state[...] = piece
        else:
            state[...] += piece
    any_ended = jnp.sum(jnp.where(used, 1.0, 0.0), axis=0, keepdims=True)
    through = jnp.where(any_ended > 0.0, 0.0, jnp.exp(total))
    link[0] = jnp.broadcast_to(through, (1, TILE))

    pl.semaphore_wait(barrier, RING + groups - 2)

    def x_copies(hop):
        to = (x + hop) % RING
        device = (z * RING + to, head)
        rows = pl.ds(pl.multiple_of(to * quarter, quarter), quarter)
        return (
            pltpu.make_async_remote_copy(
                state.at[rows], x_state.at[x], sem_xs.at[hop], sem_xr.at[x], device, MESH
            ),
            pltpu.make_async_remote_copy(
                link.at[0], x_link.at[x], sem_xls.at[hop], sem_xlr.at[x], device, MESH
            ),
        )

    for hop in (2, 1, 3):
        for copy in x_copies(hop):
            copy.start()
    mine = pl.ds(pl.multiple_of(x * quarter, quarter), quarter)
    x_state[x] = state[mine, :]
    x_link[x] = link[0]

    for t in range(tiles):
        cum_col = spread_col(cum_row[t])
        seg_col = spread_col(seg_row[t])
        queries = q_ref[pl.ds(t * TILE, TILE), :]
        part = None
        for j in range(t + 1):
            cols = pl.ds(j * TILE, TILE)
            scores = jnp.dot(queries, raw_t[:, cols], preferred_element_type=F32)
            allowed = seg_col == seg_row[j]
            if j == t:
                allowed = allowed & (
                    lax.broadcasted_iota(jnp.int32, (TILE, TILE), 0)
                    >= lax.broadcasted_iota(jnp.int32, (TILE, TILE), 1)
                )
            damping = jnp.exp(jnp.where(allowed, cum_col - cum_row[j], -jnp.inf))
            term = jnp.dot(
                (scores * damping).astype(BF16), v_ref[cols, :], preferred_element_type=F32
            )
            part = term if part is None else part + term
        mixed_ref[pl.ds(t * TILE, TILE), :] = part

    for hop in range(1, RING):
        sender = (x + hop) % RING
        pltpu.make_async_remote_copy(
            x_state.at[sender], x_state.at[sender], sem_xs.at[hop], sem_xr.at[sender], (place, head), MESH
        ).wait_recv()
        pltpu.make_async_remote_copy(
            x_link.at[sender], x_link.at[sender], sem_xls.at[hop], sem_xlr.at[sender], (place, head), MESH
        ).wait_recv()
    group_state, group_link = x_state[0], x_link[0]
    for n in range(1, RING):
        group_state = group_state * x_link[n] + x_state[n]
        group_link = group_link * x_link[n]
    z_out[...] = group_state.astype(BF16)
    z_link_out[0] = group_link

    def z_copies(hop):
        device = ((z + hop) * RING + x, head)
        return (
            pltpu.make_async_remote_copy(
                z_out, z_state.at[z], sem_zs.at[hop], sem_zr.at[z], device, MESH
            ),
            pltpu.make_async_remote_copy(
                z_link_out.at[0], z_link.at[z], sem_zls.at[hop], sem_zlr.at[z], device, MESH
            ),
        )

    for hop in sorted(range(1, groups), key=lambda n: -min(n, groups - n)):

        @pl.when(z + hop < groups)
        def _():
            for copy in z_copies(hop):
                copy.start()

    own_all = jnp.concatenate(own_row, axis=1)
    batch = lhs.shape[0] // depth

    def slot_group(n, carry):
        for b in range(batch):
            number = (n * batch + b).astype(F32)
            mask = jnp.where(own_all == number, 1.0, 0.0).astype(BF16)
            lhs[pl.ds(b * depth, depth), :] = scaled_t[...] * mask
        result = jnp.dot(lhs[...], v_ref[...], preferred_element_type=F32)
        slots_ref[pl.ds(n * batch, batch)] = result.astype(BF16).reshape(
            batch, depth, v_ref.shape[1]
        )
        return carry

    lax.fori_loop(0, owners // batch, slot_group, 0)
    leading = jnp.where((jnp.concatenate(seg_row, axis=1) == 0.0) & (own_all >= 0.0), 1.0, 0.0)
    first_state[...] = jnp.dot(
        scaled_t[...] * leading.astype(BF16), v_ref[...], preferred_element_type=F32
    )

    def z_turn(n, total_state):
        pltpu.make_async_remote_copy(
            z_out, z_state.at[n], sem_zs.at[0], sem_zr.at[n], (place, head), MESH
        ).wait_recv()
        pltpu.make_async_remote_copy(
            z_link_out.at[0], z_link.at[n], sem_zls.at[0], sem_zlr.at[n], (place, head), MESH
        ).wait_recv()
        return total_state * z_link[n] + z_state[n].astype(F32)

    reached = lax.fori_loop(0, z, z_turn, jnp.zeros((quarter, v_ref.shape[1]), F32))
    for n in range(RING):
        back_out[n] = reached
        reached = reached * x_link[n] + x_state[n]

    def back_copy(hop):
        to = (x + hop) % RING
        return pltpu.make_async_remote_copy(
            back_out.at[to],
            back_in.at[x],
            sem_bs.at[hop],
            sem_br.at[x],
            (z * RING + to, head),
            MESH,
        )

    for hop in (2, 1, 3):
        back_copy(hop).start()
    back_in[x] = back_out[x]
    for hop in range(1, RING):
        for copy in x_copies(hop):
            copy.wait_send()
    for hop in range(1, groups):

        @pl.when(z + hop < groups)
        def _():
            for copy in z_copies(hop):
                copy.wait_send()

    for hop in range(1, RING):
        sender = (x + hop) % RING
        pltpu.make_async_remote_copy(
            back_out.at[0], back_in.at[sender], sem_bs.at[hop], sem_br.at[sender], (place, head), MESH
        ).wait_recv()
    for hop in range(1, RING):
        back_copy(hop).wait_send()

    carry = back_in[...].reshape(depth, v_ref.shape[1])
    leads = ends[0:1, :]
    lead_level = at_end[0:1, :]
    lead_owner = jnp.where(leads > 0.0, owner[0:1, :], -1.0)
    lead = (first_state[...] + jnp.exp(lead_level) * carry).astype(BF16)

    def finish(n, none):
        slots_ref[n] = jnp.where(
            jnp.broadcast_to(lead_owner == n.astype(F32), lead.shape), lead, slots_ref[n]
        )
        return none

    lax.fori_loop(0, owners, finish, 0, unroll=4)
    high = carry.astype(BF16)
    low = (carry - high.astype(F32)).astype(BF16)
    for t in range(tiles):
        rows = pl.ds(t * TILE, TILE)
        queries = q_ref[rows, :]
        reach = spread_col(jnp.where(seg_row[t] == 0.0, jnp.exp(cum_row[t]), 0.0))
        brought = jnp.dot(queries, high, preferred_element_type=F32) + jnp.dot(
            queries, low, preferred_element_type=F32
        )
        out = mixed_ref[rows, :] + brought * reach
        mixed_ref[rows, :] = out
        squares_ref[pl.ds(t, 1), :] = jnp.sum(jnp.transpose(out * out), axis=0, keepdims=True)


def norm(count, mixed_ref, squares_ref, gain_ref, page_ref, first_ref, attended_ref, source_ref):
    tiles = squares_ref.shape[0]
    for t in range(tiles):
        rows = pl.ds(t * TILE, TILE)
        scale = spread_col(lax.rsqrt(squares_ref[pl.ds(t, 1), :] / count + EPS))
        attended_ref[rows, :] = (mixed_ref[rows, :] * scale * gain_ref[...]).astype(BF16)
    senders, docs = page_ref.shape
    pages = lax.broadcasted_iota(jnp.int32, (senders, docs), 0) + first_ref[0]

    def look(n, found):
        row = page_ref[pl.ds(n, 1), :]
        return jnp.where(row == pages, n.astype(F32), found)

    found = lax.fori_loop(0, senders, look, jnp.full((senders, docs), -1.0, F32), unroll=4)
    found = jnp.max(found, axis=1, keepdims=True)
    eye = lax.broadcasted_iota(jnp.int32, (senders, senders), 0) == lax.broadcasted_iota(
        jnp.int32, (senders, senders), 1
    )
    source_ref[...] = jnp.sum(
        jnp.where(eye, jnp.broadcast_to(found, (senders, senders)), 0.0), axis=0, keepdims=True
    ).astype(jnp.int32)


def settle(source_ref, incoming_ref, cache_ref, blank, sem):
    blank[...] = jnp.zeros_like(blank)
    pages = cache_ref.shape[0]

    def begin(n, none):
        source = source_ref[0, n]

        @pl.when(source >= 0)
        def _():
            pltpu.make_async_copy(incoming_ref.at[source], cache_ref.at[n], sem).start()

        @pl.when(source < 0)
        def _():
            pltpu.make_async_copy(blank, cache_ref.at[n], sem).start()

        return none

    lax.fori_loop(0, pages, begin, 0)
    pltpu.make_async_copy(incoming_ref, cache_ref, sem).wait()


VMEM = pl.BlockSpec(memory_space=pltpu.VMEM)
SMEM = pl.BlockSpec(memory_space=pltpu.SMEM)
LIMIT = 48 << 20


def shards(query_rows, key_rows, value_rows, log_gate, norm_gain, doc_ends, doc_page):
    tokens, heads, depth = query_rows.shape
    width = value_rows.shape[2]
    devices = lax.axis_size("seq")
    bounds = doc_ends.shape[0]
    groups = devices // RING
    quarter = depth // RING
    table = doc_page.reshape(devices, bounds)
    dma = pltpu.SemaphoreType.DMA
    slots, mixed, squares = pl.pallas_call(
        functools.partial(front, groups),
        out_shape=(
            jax.ShapeDtypeStruct((devices, depth, width), BF16),
            jax.ShapeDtypeStruct((tokens, width), F32),
            jax.ShapeDtypeStruct((tokens // TILE, TILE), F32),
        ),
        in_specs=[VMEM] * 6,
        out_specs=(VMEM,) * 3,
        scratch_shapes=[
            pltpu.VMEM((depth, tokens), BF16),
            pltpu.VMEM((depth, tokens), BF16),
            pltpu.VMEM((8 * depth, tokens), BF16),
            pltpu.VMEM((depth, width), F32),
            pltpu.VMEM((1, 1, TILE), F32),
            pltpu.VMEM((RING, quarter, width), F32),
            pltpu.VMEM((RING, 1, TILE), F32),
            pltpu.VMEM((quarter, width), BF16),
            pltpu.VMEM((1, 1, TILE), F32),
            pltpu.VMEM((groups, quarter, width), BF16),
            pltpu.VMEM((groups, 1, TILE), F32),
            pltpu.VMEM((RING, quarter, width), F32),
            pltpu.VMEM((RING, quarter, width), F32),
            pltpu.VMEM((depth, width), F32),
            dma((RING,)),
            dma((RING,)),
            dma((RING,)),
            dma((RING,)),
            dma((groups,)),
            dma((groups,)),
            dma((groups,)),
            dma((groups,)),
            dma((RING,)),
            dma((RING,)),
        ],
        compiler_params=pltpu.CompilerParams(
            collective_id=0, has_side_effects=True, vmem_limit_bytes=LIMIT
        ),
        name="front",
    )(
        query_rows.reshape(tokens, depth),
        key_rows.reshape(tokens, depth),
        value_rows.reshape(tokens, width),
        log_gate.reshape(tokens // TILE, TILE),
        doc_ends.reshape(1, bounds),
        table,
    )
    incoming = lax.all_to_all(slots, "seq", split_axis=0, concat_axis=0, tiled=True)
    squares = lax.psum(squares, "head")
    first_page = (lax.axis_index("seq") * devices).astype(jnp.int32).reshape(1)
    attended, source = pl.pallas_call(
        functools.partial(norm, heads * lax.axis_size("head") * width),
        out_shape=(
            jax.ShapeDtypeStruct((tokens, width), BF16),
            jax.ShapeDtypeStruct((1, devices), jnp.int32),
        ),
        in_specs=[VMEM, VMEM, VMEM, VMEM, SMEM],
        out_specs=(VMEM, VMEM),
        name="norm",
    )(mixed, squares, norm_gain, table, first_page)
    cache = pl.pallas_call(
        settle,
        out_shape=jax.ShapeDtypeStruct((devices, depth, width), BF16),
        in_specs=[SMEM, VMEM],
        out_specs=pl.BlockSpec(memory_space=pltpu.HBM),
        scratch_shapes=[pltpu.VMEM((depth, width), BF16), pltpu.SemaphoreType.DMA],
        name="settle",
    )(source, incoming)
    return attended.reshape(tokens, heads, width), cache.reshape(devices, heads, depth, width)


def solution(mesh):
    placed = (
        P("seq", "head", None),
        P("seq", "head", None),
        P("seq", "head", None),
        P("head", "seq"),
        P("head", None),
        P("seq"),
        P(),
    )
    return jax.shard_map(
        shards,
        mesh=mesh,
        in_specs=placed,
        out_specs=(P("seq", "head", None), P("seq", "head", None, None)),
        check_vma=False,
    )
```

```python
import functools

import jax
import jax.numpy as jnp
from jax import lax
from jax.experimental import pallas as pl
from jax.experimental.pallas import tpu as pltpu
from jax.sharding import PartitionSpec as P

EPS = 1e-05
RING = 4
TILE = 128
MESH = pl.DeviceIdType.MESH
F32 = jnp.float32
BF16 = jnp.bfloat16


def row_to_col(row):
    n = row.shape[1]
    eye = lax.broadcasted_iota(jnp.int32, (n, n), 0) == lax.broadcasted_iota(jnp.int32, (n, n), 1)
    return jnp.sum(jnp.where(eye, jnp.broadcast_to(row, (n, n)), 0.0), axis=1, keepdims=True)


def spread_col(row):
    n = row.shape[1]
    return jnp.transpose(jnp.broadcast_to(row, (n, n)))


def running_sum(gates):
    rows, lanes = gates.shape
    lane = lax.broadcasted_iota(jnp.int32, gates.shape, 1)
    sub = lax.broadcasted_iota(jnp.int32, gates.shape, 0)
    total = gates
    step = 1
    while step < lanes:
        total = total + jnp.where(lane >= step, pltpu.roll(total, step, 1), 0.0)
        step *= 2
    last = jnp.broadcast_to(total[:, lanes - 1 :], gates.shape)
    before = jnp.where(sub >= 1, pltpu.roll(last, 1, 0), 0.0)
    step = 1
    while step < rows:
        before = before + jnp.where(sub >= step, pltpu.roll(before, step, 0), 0.0)
        step *= 2
    return total + before


def order_of(groups):
    half = groups // 2
    order = [half]
    for hop in range(half - 1, 0, -1):
        order += [hop, -hop]
    return order + [0]


def whole(
    groups,
    heads,
    count,
    q_hbm,
    k_hbm,
    v_hbm,
    gate_hbm,
    ends_hbm,
    table_hbm,
    gain_hbm,
    incoming,
    attended_ref,
    source_ref,
    q_ref,
    k_ref,
    v_ref,
    gate_ref,
    table_ref,
    ends_ref,
    gain_ref,
    slots,
    relay,
    mixed,
    cum_rows,
    seg_rows,
    own_rows,
    squares,
    head_squares,
    raw_t,
    scaled_t,
    lhs,
    state,
    link,
    x_state,
    x_link,
    z_out,
    z_link_out,
    z_state,
    z_link,
    back_out,
    back_in,
    first_state,
    sem_in,
    sem_xs,
    sem_xr,
    sem_xls,
    sem_xlr,
    sem_zs,
    sem_zr,
    sem_zls,
    sem_zlr,
    sem_bs,
    sem_br,
    sem_hs,
    sem_hr,
    sem_os,
    sem_or,
    sem_rs,
    sem_rr,
    sem_fs,
):
    place = lax.axis_index("seq")
    head = lax.axis_index("head")
    z, x = place // RING, place % RING
    tokens, depth = k_ref.shape
    tiles = tokens // TILE
    docs = ends_ref.shape[1]
    owners = slots.shape[0]
    quarter = depth // RING

    loads = [
        pltpu.make_async_copy(source, target, sem_in.at[n])
        for n, (source, target) in enumerate(
            (
                (gate_hbm, gate_ref),
                (table_hbm, table_ref),
                (k_hbm, k_ref),
                (v_hbm, v_ref),
                (q_hbm, q_ref),
                (ends_hbm, ends_ref),
                (gain_hbm, gain_ref),
            )
        )
    ]
    for load in loads:
        load.start()

    barrier = pltpu.get_barrier_semaphore()

    def greet_seq(n, none):
        device = ((place + n) % owners, head)
        pl.semaphore_signal(barrier, inc=1, device_id=device, device_id_type=MESH)
        return none

    def greet_head(n, none):
        device = (place, (head + n) % heads)
        pl.semaphore_signal(barrier, inc=1, device_id=device, device_id_type=MESH)
        return none

    lax.fori_loop(1, owners, greet_seq, 0)
    lax.fori_loop(1, heads, greet_head, 0)

    loads[0].wait()
    loads[1].wait()
    loads[5].wait()
    cum = running_sum(gate_ref[...])
    cum_rows[...] = cum
    ends = row_to_col(ends_ref[...].astype(F32))
    fold = TILE // docs
    pages = jnp.broadcast_to(table_ref[pl.ds(place // fold, 1), :], (8, TILE))
    aligned = pages
    for n in range(1, fold):
        here = jnp.full((8, TILE), place % fold, jnp.int32) == n
        aligned = jnp.where(here, pltpu.roll(pages, TILE - n * docs, 1), aligned)
    owner = row_to_col((aligned[0:1, :docs] >> (owners.bit_length() - 1)).astype(F32))
    used = ends > 0.0
    lane = lax.broadcasted_iota(jnp.int32, (docs, TILE), 1).astype(F32)
    doc = lax.broadcasted_iota(jnp.int32, (docs, TILE), 0).astype(F32)
    cum_row = [cum[t : t + 1, :] for t in range(tiles)]
    total = cum[tiles - 1 :, TILE - 1 :]
    seg_row = []
    at_end = jnp.zeros((docs, 1), F32)
    for t in range(tiles):
        position = lane + float(t * TILE)
        seg_row.append(
            jnp.sum(jnp.where(used & (ends <= position), 1.0, 0.0), axis=0, keepdims=True)
        )
        seg_rows[pl.ds(t, 1), :] = seg_row[t]
        at_end = at_end + jnp.sum(
            jnp.where(position == ends - 1.0, jnp.broadcast_to(cum_row[t], position.shape), 0.0),
            axis=1,
            keepdims=True,
        )
    loads[2].wait()
    loads[3].wait()
    for t in range(tiles):
        inside = (jnp.broadcast_to(seg_row[t], doc.shape) == doc) & used
        done = jnp.sum(jnp.where(inside, 1.0, 0.0), axis=0, keepdims=True)
        stop = jnp.sum(jnp.where(inside, at_end, 0.0), axis=0, keepdims=True)
        owned = jnp.sum(jnp.where(inside, owner, 0.0), axis=0, keepdims=True)
        stop = jnp.where(done > 0.0, stop, total)
        cols = pl.ds(t * TILE, TILE)
        own_rows[:, cols] = jnp.where(done > 0.0, owned, -1.0)
        keep = jnp.where(done > 0.0, 0.0, 1.0)
        weight = jnp.exp(stop - cum_row[t])
        turned = jnp.transpose(k_ref[cols, :].astype(F32))
        raw_t[:, cols] = turned.astype(BF16)
        turned = turned * weight
        high = turned.astype(BF16)
        scaled_t[:, cols] = high
        low = ((turned - high.astype(F32)) * keep).astype(BF16)
        values = v_ref[cols, :]
        piece = jnp.dot((high.astype(F32) * keep).astype(BF16), values, preferred_element_type=F32)
        piece = piece + jnp.dot(low, values, preferred_element_type=F32)
        if t == 0:
            state[...] = piece
        else:
            state[...] += piece
    any_ended = jnp.sum(jnp.where(used, 1.0, 0.0), axis=0, keepdims=True)
    through = jnp.where(any_ended > 0.0, 0.0, jnp.exp(total))
    link[0] = jnp.broadcast_to(through, (1, TILE))

    pl.semaphore_wait(barrier, owners + heads - 2)

    def x_copies(hop):
        to = (x + hop) % RING
        device = (z * RING + to, head)
        rows = pl.ds(pl.multiple_of(to * quarter, quarter), quarter)
        return (
            pltpu.make_async_remote_copy(
                state.at[rows], x_state.at[x], sem_xs.at[hop], sem_xr.at[x], device, MESH
            ),
            pltpu.make_async_remote_copy(
                link.at[0], x_link.at[x], sem_xls.at[hop], sem_xlr.at[x], device, MESH
            ),
        )

    def arrived(target, sem):
        pltpu.make_async_remote_copy(
            target, target, sem_in.at[0], sem, (place, head), MESH
        ).wait_recv()

    for hop in (2, 1, 3):
        for copy in x_copies(hop):
            copy.start()
    mine = pl.ds(pl.multiple_of(x * quarter, quarter), quarter)
    x_state[x] = state[mine, :]
    x_link[x] = link[0]
    for hop in range(1, RING):
        sender = (x + hop) % RING
        arrived(x_state.at[sender], sem_xr.at[sender])
        arrived(x_link.at[sender], sem_xlr.at[sender])
    group_state, group_link = x_state[0], x_link[0]
    for n in range(1, RING):
        group_state = group_state * x_link[n] + x_state[n]
        group_link = group_link * x_link[n]
    z_out[...] = group_state.astype(BF16)
    z_link_out[0] = group_link

    def z_copies(hop):
        device = ((z + hop) * RING + x, head)
        return (
            pltpu.make_async_remote_copy(
                z_out, z_state.at[z], sem_zs.at[hop], sem_zr.at[z], device, MESH
            ),
            pltpu.make_async_remote_copy(
                z_link_out.at[0], z_link.at[z], sem_zls.at[hop], sem_zlr.at[z], device, MESH
            ),
        )

    for hop in sorted(range(1, groups), key=lambda n: -min(n, groups - n)):

        @pl.when(z + hop < groups)
        def _():
            for copy in z_copies(hop):
                copy.start()

    own_all = own_rows[...]
    batch = lhs.shape[0] // depth

    def slot_group(n, carry):
        for b in range(batch):
            number = (n * batch + b).astype(F32)
            mask = jnp.where(own_rows[...] == number, 1.0, 0.0).astype(BF16)
            lhs[pl.ds(b * depth, depth), :] = scaled_t[...] * mask
        result = jnp.dot(lhs[...], v_ref[...], preferred_element_type=F32)
        slots[pl.ds(n * batch, batch)] = result.astype(BF16).reshape(batch, depth, v_ref.shape[1])
        return carry

    lax.fori_loop(0, owners // batch, slot_group, 0)
    leading = jnp.where((jnp.concatenate(seg_row, axis=1) == 0.0) & (own_all >= 0.0), 1.0, 0.0)
    first_state[...] = jnp.dot(
        scaled_t[...] * leading.astype(BF16), v_ref[...], preferred_element_type=F32
    )

    def z_turn(n, total_state):
        arrived(z_state.at[n], sem_zr.at[n])
        arrived(z_link.at[n], sem_zlr.at[n])
        return total_state * z_link[n] + z_state[n].astype(F32)

    reached = lax.fori_loop(0, z, z_turn, jnp.zeros((quarter, v_ref.shape[1]), F32))
    for n in range(RING):
        back_out[n] = reached
        reached = reached * x_link[n] + x_state[n]

    def back_copy(hop):
        to = (x + hop) % RING
        return pltpu.make_async_remote_copy(
            back_out.at[to],
            back_in.at[x],
            sem_bs.at[hop],
            sem_br.at[x],
            (z * RING + to, head),
            MESH,
        )

    for hop in (2, 1, 3):
        back_copy(hop).start()
    back_in[x] = back_out[x]
    for hop in range(1, RING):
        sender = (x + hop) % RING
        arrived(back_in.at[sender], sem_br.at[sender])

    carry = back_in[...].reshape(depth, v_ref.shape[1])
    lead_owner = jnp.where(ends[0:1, :] > 0.0, owner[0:1, :], -1.0)
    lead = (first_state[...] + jnp.exp(at_end[0:1, :]) * carry).astype(BF16)

    half, step_off = groups // 2, groups // 4
    relays = tuple((n, -1 if n % 2 == 0 else 1) for n in range(RING)) if step_off else ()
    order = order_of(groups)
    early = len(order) * 9 // 16

    def target(hop, turn):
        return ((z + hop + groups) % groups) * RING + (x + turn) % RING

    def finish(hop):
        def one(turn, none):
            n = target(hop, turn)
            slots[n] = jnp.where(
                jnp.broadcast_to(lead_owner == n.astype(F32), lead.shape), lead, slots[n]
            )
            return none

        lax.fori_loop(0, RING, one, 0)

    def direct(hop, turn):
        n = target(hop, turn)
        return pltpu.make_async_remote_copy(
            slots.at[n], incoming.at[place], sem_os.at[n], sem_or.at[place], (n, head), MESH
        )

    def first_leg(r):
        turn, way = relays[r]
        via = target(way * step_off, 0)
        return pltpu.make_async_remote_copy(
            slots.at[target(half, turn)],
            relay.at[r],
            sem_rs.at[r],
            sem_rr.at[r],
            (via, head),
            MESH,
        )

    def second_leg(r):
        turn, way = relays[r]
        source = target(-way * step_off, 0)
        return pltpu.make_async_remote_copy(
            relay.at[r],
            incoming.at[source],
            sem_fs.at[r],
            sem_or.at[source],
            (target(way * step_off, turn), head),
            MESH,
        )

    def fire(hop):
        if hop == half and relays:
            for r in range(len(relays)):
                first_leg(r).start()
            return

        def one(turn, none):
            direct(hop, turn).start()
            return none

        lax.fori_loop(1 if hop == 0 else 0, RING, one, 0)

    finish(order[0])
    for n, hop in enumerate(order):
        if n + 1 < len(order):
            finish(order[n + 1])
        if n < early:
            fire(hop)

    incoming[place] = slots[place]
    loads[4].wait()
    loads[6].wait()
    high = carry.astype(BF16)
    low = (carry - high.astype(F32)).astype(BF16)
    later = lax.broadcasted_iota(jnp.int32, (TILE, TILE), 0) - lax.broadcasted_iota(
        jnp.int32, (TILE, TILE), 1
    )

    def attend(t, none):
        rows = pl.ds(pl.multiple_of(t * TILE, TILE), TILE)
        queries = q_ref[rows, :]
        my_cum = cum_rows[pl.ds(t, 1), :]
        my_seg = seg_rows[pl.ds(t, 1), :]
        cum_col = spread_col(my_cum)
        seg_col = spread_col(my_seg)
        reach = spread_col(jnp.where(my_seg == 0.0, jnp.exp(my_cum), 0.0))
        brought = jnp.dot(queries, high, preferred_element_type=F32) + jnp.dot(
            queries, low, preferred_element_type=F32
        )

        def look(j, part):
            cols = pl.ds(pl.multiple_of(j * TILE, TILE), TILE)
            scores = jnp.dot(queries, raw_t[:, cols], preferred_element_type=F32)
            allowed = (seg_col == seg_rows[pl.ds(j, 1), :]) & (later + (t - j) * TILE >= 0)
            damping = jnp.exp(jnp.where(allowed, cum_col - cum_rows[pl.ds(j, 1), :], -jnp.inf))
            return part + jnp.dot(
                (scores * damping).astype(BF16), v_ref[cols, :], preferred_element_type=F32
            )

        out = lax.fori_loop(0, t + 1, look, brought * reach)
        mixed[rows, :] = out
        squares[pl.ds(t, 1), :] = jnp.sum(jnp.transpose(out * out), axis=0, keepdims=True)
        return none

    lax.fori_loop(0, tiles, attend, 0)

    def square_copy(n):
        return pltpu.make_async_remote_copy(
            squares,
            head_squares.at[head],
            sem_hs.at[n],
            sem_hr.at[head],
            (place, (head + n) % heads),
            MESH,
        )

    def send_square(n, none):
        square_copy(n).start()
        return none

    lax.fori_loop(1, heads, send_square, 0)
    head_squares[head] = squares[...]

    for r in range(len(relays)):
        arrived(relay.at[r], sem_rr.at[r])
        second_leg(r).start()
    for hop in order[early:]:
        fire(hop)

    fold_rows = table_ref.shape[0]
    page_lane = lax.broadcasted_iota(jnp.int32, (owners, TILE), 1)
    wanted = lax.broadcasted_iota(jnp.int32, (owners, TILE), 0) + place * owners
    which = (page_lane // docs).astype(F32)

    def search(n, found):
        row = table_ref[pl.ds(n, 1), :]
        return jnp.where(row == wanted, which + (n * fold).astype(F32), found)

    found = lax.fori_loop(0, fold_rows, search, jnp.full((owners, TILE), -1.0, F32))
    found = jnp.max(found, axis=1, keepdims=True)
    eye = lax.broadcasted_iota(jnp.int32, (owners, owners), 0) == lax.broadcasted_iota(
        jnp.int32, (owners, owners), 1
    )
    source_ref[...] = jnp.sum(
        jnp.where(eye, jnp.broadcast_to(found, (owners, owners)), 0.0), axis=0, keepdims=True
    ).astype(jnp.int32)

    def take_square(n, none):
        sender = (head + n) % heads
        arrived(head_squares.at[sender], sem_hr.at[sender])
        return none

    lax.fori_loop(1, heads, take_square, 0)
    energy = head_squares[0]
    for n in range(1, heads):
        energy = energy + head_squares[n]
    cum_rows[...] = lax.rsqrt(energy / count + EPS)

    def normed(t, none):
        rows = pl.ds(pl.multiple_of(t * TILE, TILE), TILE)
        scale = spread_col(cum_rows[pl.ds(t, 1), :])
        attended_ref[rows, :] = (mixed[rows, :] * scale * gain_ref[...]).astype(BF16)
        return none

    lax.fori_loop(0, tiles, normed, 0)

    for hop in range(1, RING):
        for copy in x_copies(hop):
            copy.wait_send()
        back_copy(hop).wait_send()
    for hop in range(1, groups):

        @pl.when(z + hop < groups)
        def _():
            for copy in z_copies(hop):
                copy.wait_send()

    def sent_square(n, none):
        square_copy(n).wait_send()
        return none

    lax.fori_loop(1, heads, sent_square, 0)
    for hop in order:
        if hop == half and relays:
            for r in range(len(relays)):
                first_leg(r).wait_send()
            continue

        def sent(turn, none):
            direct(hop, turn).wait_send()
            return none

        lax.fori_loop(1 if hop == 0 else 0, RING, sent, 0)

    def landed(n, none):
        sender = (place + n) % owners
        arrived(incoming.at[sender], sem_or.at[sender])
        return none

    lax.fori_loop(1, owners, landed, 0)
    for r in range(len(relays)):
        second_leg(r).wait_send()


def settle(source_ref, incoming_ref, attended_in, cache_ref, attended_ref, blank, sem, sem_two):
    rows = pltpu.make_async_copy(attended_in, attended_ref, sem_two)
    rows.start()
    blank[...] = jnp.zeros_like(blank)
    pages = cache_ref.shape[0]

    def begin(n, none):
        source = source_ref[0, n]

        @pl.when(source >= 0)
        def _():
            pltpu.make_async_copy(incoming_ref.at[source], cache_ref.at[n], sem).start()

        @pl.when(source < 0)
        def _():
            pltpu.make_async_copy(blank, cache_ref.at[n], sem).start()

        return none

    lax.fori_loop(0, pages, begin, 0, unroll=4)
    pltpu.make_async_copy(incoming_ref, cache_ref, sem).wait()
    rows.wait()


VMEM = pl.BlockSpec(memory_space=pltpu.VMEM)
SMEM = pl.BlockSpec(memory_space=pltpu.SMEM)
HBM = pl.BlockSpec(memory_space=pltpu.HBM)


def in_hbm(array):
    return pltpu.with_memory_space_constraint(array, pltpu.HBM)


def shards(query_rows, key_rows, value_rows, log_gate, norm_gain, doc_ends, doc_page):
    tokens, heads, depth = query_rows.shape
    width = value_rows.shape[2]
    devices, ranks = lax.axis_size("seq"), lax.axis_size("head")
    bounds = doc_ends.shape[0]
    groups = devices // RING
    quarter = depth // RING
    tiles = tokens // TILE
    table = doc_page.reshape(devices * bounds // TILE, TILE)
    dma = pltpu.SemaphoreType.DMA
    incoming, attended, source = pl.pallas_call(
        functools.partial(whole, groups, ranks, heads * ranks * width),
        out_shape=(
            jax.ShapeDtypeStruct((devices, depth, width), BF16),
            jax.ShapeDtypeStruct((tokens, width), BF16),
            jax.ShapeDtypeStruct((1, devices), jnp.int32),
        ),
        in_specs=[HBM] * 7,
        out_specs=(VMEM, VMEM, VMEM),
        scratch_shapes=[
            pltpu.VMEM((tokens, depth), BF16),
            pltpu.VMEM((tokens, depth), BF16),
            pltpu.VMEM((tokens, width), BF16),
            pltpu.VMEM((tiles, TILE), F32),
            pltpu.VMEM(table.shape, jnp.int32),
            pltpu.VMEM((1, bounds), jnp.int32),
            pltpu.VMEM((1, width), F32),
            pltpu.VMEM((devices, depth, width), BF16),
            pltpu.VMEM((RING, depth, width), BF16),
            pltpu.VMEM((tokens, width), F32),
            pltpu.VMEM((tiles, TILE), F32),
            pltpu.VMEM((tiles, TILE), F32),
            pltpu.VMEM((1, tokens), F32),
            pltpu.VMEM((tiles, TILE), F32),
            pltpu.VMEM((ranks, tiles, TILE), F32),
            pltpu.VMEM((depth, tokens), BF16),
            pltpu.VMEM((depth, tokens), BF16),
            pltpu.VMEM((8 * depth, tokens), BF16),
            pltpu.VMEM((depth, width), F32),
            pltpu.VMEM((1, 1, TILE), F32),
            pltpu.VMEM((RING, quarter, width), F32),
            pltpu.VMEM((RING, 1, TILE), F32),
            pltpu.VMEM((quarter, width), BF16),
            pltpu.VMEM((1, 1, TILE), F32),
            pltpu.VMEM((groups, quarter, width), BF16),
            pltpu.VMEM((groups, 1, TILE), F32),
            pltpu.VMEM((RING, quarter, width), F32),
            pltpu.VMEM((RING, quarter, width), F32),
            pltpu.VMEM((depth, width), F32),
            dma((7,)),
            dma((RING,)),
            dma((RING,)),
            dma((RING,)),
            dma((RING,)),
            dma((groups,)),
            dma((groups,)),
            dma((groups,)),
            dma((groups,)),
            dma((RING,)),
            dma((RING,)),
            dma((ranks,)),
            dma((ranks,)),
            dma((devices,)),
            dma((devices,)),
            dma((RING,)),
            dma((RING,)),
            dma((RING,)),
        ],
        compiler_params=pltpu.CompilerParams(
            collective_id=0, has_side_effects=True, vmem_limit_bytes=40 << 20
        ),
        name="whole",
    )(
        in_hbm(query_rows.reshape(tokens, depth)),
        in_hbm(key_rows.reshape(tokens, depth)),
        in_hbm(value_rows.reshape(tokens, width)),
        in_hbm(log_gate.reshape(tiles, TILE)),
        in_hbm(doc_ends.reshape(1, bounds)),
        in_hbm(table),
        in_hbm(norm_gain),
    )
    cache, attended = pl.pallas_call(
        settle,
        out_shape=(
            jax.ShapeDtypeStruct((devices, depth, width), BF16),
            jax.ShapeDtypeStruct((tokens, width), BF16),
        ),
        in_specs=[SMEM, VMEM, VMEM],
        out_specs=(HBM, HBM),
        scratch_shapes=[
            pltpu.VMEM((depth, width), BF16),
            pltpu.SemaphoreType.DMA,
            pltpu.SemaphoreType.DMA,
        ],
        compiler_params=pltpu.CompilerParams(vmem_limit_bytes=8 << 20),
        name="settle",
    )(source, incoming, attended)
    return attended.reshape(tokens, heads, width), cache.reshape(devices, heads, depth, width)


def solution(mesh):
    placed = (
        P("seq", "head", None),
        P("seq", "head", None),
        P("seq", "head", None),
        P("head", "seq"),
        P("head", None),
        P("seq"),
        P(),
    )
    return jax.shard_map(
        shards,
        mesh=mesh,
        in_specs=placed,
        out_specs=(P("seq", "head", None), P("seq", "head", None, None)),
        check_vma=False,
    )
```

```python
import functools

import jax
import jax.numpy as jnp
from jax import lax
from jax.experimental import pallas as pl
from jax.experimental.pallas import tpu as pltpu
from jax.sharding import PartitionSpec as P

EPS = 1e-05
RING = 4
TILE = 128
MESH = pl.DeviceIdType.MESH
F32 = jnp.float32
BF16 = jnp.bfloat16


def row_to_col(row):
    n = row.shape[1]
    eye = lax.broadcasted_iota(jnp.int32, (n, n), 0) == lax.broadcasted_iota(jnp.int32, (n, n), 1)
    return jnp.sum(jnp.where(eye, jnp.broadcast_to(row, (n, n)), 0.0), axis=1, keepdims=True)


def spread_col(row):
    n = row.shape[1]
    return jnp.transpose(jnp.broadcast_to(row, (n, n)))


def running_sum(gates):
    rows, lanes = gates.shape
    lane = lax.broadcasted_iota(jnp.int32, gates.shape, 1)
    sub = lax.broadcasted_iota(jnp.int32, gates.shape, 0)
    total = gates
    step = 1
    while step < lanes:
        total = total + jnp.where(lane >= step, pltpu.roll(total, step, 1), 0.0)
        step *= 2
    last = jnp.broadcast_to(total[:, lanes - 1 :], gates.shape)
    before = jnp.where(sub >= 1, pltpu.roll(last, 1, 0), 0.0)
    step = 1
    while step < rows:
        before = before + jnp.where(sub >= step, pltpu.roll(before, step, 0), 0.0)
        step *= 2
    return total + before


def order_of(groups):
    half = groups // 2
    order = [half]
    for hop in range(half - 1, 0, -1):
        order += [hop, -hop]
    return order + [0]


def whole(
    groups,
    heads,
    count,
    q_hbm,
    k_hbm,
    v_hbm,
    gate_hbm,
    ends_hbm,
    table_hbm,
    gain_hbm,
    incoming,
    attended_ref,
    source_ref,
    q_ref,
    k_ref,
    v_ref,
    gate_ref,
    table_ref,
    ends_ref,
    gain_ref,
    slots,
    relay,
    mixed,
    cum_rows,
    seg_rows,
    own_rows,
    squares,
    head_out,
    head_in,
    raw_t,
    scaled_t,
    lhs,
    state,
    link,
    x_state,
    x_link,
    z_out,
    z_link_out,
    z_state,
    z_link,
    back_out,
    back_in,
    first_state,
    ready,
    sem_in,
    sem_xs,
    sem_xr,
    sem_xls,
    sem_xlr,
    sem_zs,
    sem_zr,
    sem_zls,
    sem_zlr,
    sem_bs,
    sem_br,
    sem_hs,
    sem_hr,
    sem_os,
    sem_or,
    sem_rs,
    sem_rr,
    sem_fs,
):
    place = lax.axis_index("seq")
    head = lax.axis_index("head")
    z, x = place // RING, place % RING
    tokens, depth = k_ref.shape
    tiles = tokens // TILE
    docs = ends_ref.shape[1]
    owners = slots.shape[0]
    quarter = depth // RING

    loads = [
        pltpu.make_async_copy(source, target, sem_in.at[n])
        for n, (source, target) in enumerate(
            (
                (gate_hbm, gate_ref),
                (table_hbm, table_ref),
                (k_hbm, k_ref),
                (v_hbm, v_ref),
                (q_hbm, q_ref),
                (ends_hbm, ends_ref),
                (gain_hbm, gain_ref),
            )
        )
    ]
    for load in loads:
        load.start()

    barrier = pltpu.get_barrier_semaphore()

    spans = [1 << n for n in range((heads - 1).bit_length())]

    def partner(span):
        return head + span * (1 - 2 * ((head // span) % 2))

    def greet(semaphore, device):
        pl.semaphore_signal(semaphore, inc=1, device_id=device, device_id_type=MESH)

    reach_out = sorted(range(1, groups), key=lambda n: -min(n, groups - n))
    for hop in reach_out:
        greet(barrier, (((z + hop) % groups) * RING + x, head))
    for hop in (2, 1, 3):
        greet(barrier, (z * RING + (x + hop) % RING, head))
    for span in spans:
        greet(barrier, (place, partner(span)))

    loads[0].wait()
    loads[1].wait()
    loads[5].wait()
    cum = running_sum(gate_ref[...])
    cum_rows[...] = cum
    ends = row_to_col(ends_ref[...].astype(F32))
    fold = TILE // docs
    pages = jnp.broadcast_to(table_ref[pl.ds(place // fold, 1), :], (8, TILE))
    aligned = pages
    for n in range(1, fold):
        here = jnp.full((8, TILE), place % fold, jnp.int32) == n
        aligned = jnp.where(here, pltpu.roll(pages, TILE - n * docs, 1), aligned)
    owner = row_to_col((aligned[0:1, :docs] >> (owners.bit_length() - 1)).astype(F32))
    used = ends > 0.0
    lane = lax.broadcasted_iota(jnp.int32, (docs, TILE), 1).astype(F32)
    doc = lax.broadcasted_iota(jnp.int32, (docs, TILE), 0).astype(F32)
    cum_row = [cum[t : t + 1, :] for t in range(tiles)]
    total = cum[tiles - 1 :, TILE - 1 :]
    seg_row = []
    at_end = jnp.zeros((docs, 1), F32)
    for t in range(tiles):
        position = lane + float(t * TILE)
        seg_row.append(
            jnp.sum(jnp.where(used & (ends <= position), 1.0, 0.0), axis=0, keepdims=True)
        )
        seg_rows[pl.ds(t, 1), :] = seg_row[t]
        at_end = at_end + jnp.sum(
            jnp.where(position == ends - 1.0, jnp.broadcast_to(cum_row[t], position.shape), 0.0),
            axis=1,
            keepdims=True,
        )
    loads[2].wait()
    loads[3].wait()
    for t in range(tiles):
        inside = (jnp.broadcast_to(seg_row[t], doc.shape) == doc) & used
        done = jnp.sum(jnp.where(inside, 1.0, 0.0), axis=0, keepdims=True)
        stop = jnp.sum(jnp.where(inside, at_end, 0.0), axis=0, keepdims=True)
        owned = jnp.sum(jnp.where(inside, owner, 0.0), axis=0, keepdims=True)
        stop = jnp.where(done > 0.0, stop, total)
        cols = pl.ds(t * TILE, TILE)
        own_rows[:, cols] = jnp.where(done > 0.0, owned, -1.0)
        keep = jnp.where(done > 0.0, 0.0, 1.0)
        weight = jnp.exp(stop - cum_row[t])
        turned = jnp.transpose(k_ref[cols, :].astype(F32))
        raw_t[:, cols] = turned.astype(BF16)
        turned = turned * weight
        high = turned.astype(BF16)
        scaled_t[:, cols] = high
        low = ((turned - high.astype(F32)) * keep).astype(BF16)
        values = v_ref[cols, :]
        piece = jnp.dot((high.astype(F32) * keep).astype(BF16), values, preferred_element_type=F32)
        piece = piece + jnp.dot(low, values, preferred_element_type=F32)
        if t == 0:
            state[...] = piece
        else:
            state[...] += piece
    any_ended = jnp.sum(jnp.where(used, 1.0, 0.0), axis=0, keepdims=True)
    through = jnp.where(any_ended > 0.0, 0.0, jnp.exp(total))
    link[0] = jnp.broadcast_to(through, (1, TILE))

    pl.semaphore_wait(barrier, groups + RING - 2 + len(spans))

    def x_copies(hop):
        to = (x + hop) % RING
        device = (z * RING + to, head)
        rows = pl.ds(pl.multiple_of(to * quarter, quarter), quarter)
        return (
            pltpu.make_async_remote_copy(
                state.at[rows], x_state.at[x], sem_xs.at[hop], sem_xr.at[x], device, MESH
            ),
            pltpu.make_async_remote_copy(
                link.at[0], x_link.at[x], sem_xls.at[hop], sem_xlr.at[x], device, MESH
            ),
        )

    def arrived(target, sem):
        pltpu.make_async_remote_copy(
            target, target, sem_in.at[0], sem, (place, head), MESH
        ).wait_recv()

    for hop in (2, 1, 3):
        for copy in x_copies(hop):
            copy.start()
    for hop in reach_out:
        greet(ready, (((z + hop) % groups) * RING + x, head))
    mine = pl.ds(pl.multiple_of(x * quarter, quarter), quarter)
    x_state[x] = state[mine, :]
    x_link[x] = link[0]
    for hop in range(1, RING):
        sender = (x + hop) % RING
        arrived(x_state.at[sender], sem_xr.at[sender])
        arrived(x_link.at[sender], sem_xlr.at[sender])
    group_state, group_link = x_state[0], x_link[0]
    for n in range(1, RING):
        group_state = group_state * x_link[n] + x_state[n]
        group_link = group_link * x_link[n]
    z_out[...] = group_state.astype(BF16)
    z_link_out[0] = group_link

    def z_copies(hop):
        device = ((z + hop) * RING + x, head)
        return (
            pltpu.make_async_remote_copy(
                z_out, z_state.at[z], sem_zs.at[hop], sem_zr.at[z], device, MESH
            ),
            pltpu.make_async_remote_copy(
                z_link_out.at[0], z_link.at[z], sem_zls.at[hop], sem_zlr.at[z], device, MESH
            ),
        )

    for hop in reach_out:

        @pl.when(z + hop < groups)
        def _():
            for copy in z_copies(hop):
                copy.start()

    own_all = own_rows[...]
    batch = lhs.shape[0] // depth

    def slot_group(n, carry):
        for b in range(batch):
            number = (n * batch + b).astype(F32)
            mask = jnp.where(own_rows[...] == number, 1.0, 0.0).astype(BF16)
            lhs[pl.ds(b * depth, depth), :] = scaled_t[...] * mask
        result = jnp.dot(lhs[...], v_ref[...], preferred_element_type=F32)
        slots[pl.ds(n * batch, batch)] = result.astype(BF16).reshape(batch, depth, v_ref.shape[1])
        return carry

    lax.fori_loop(0, owners // batch, slot_group, 0)
    leading = jnp.where((jnp.concatenate(seg_row, axis=1) == 0.0) & (own_all >= 0.0), 1.0, 0.0)
    first_state[...] = jnp.dot(
        scaled_t[...] * leading.astype(BF16), v_ref[...], preferred_element_type=F32
    )

    def z_turn(n, total_state):
        arrived(z_state.at[n], sem_zr.at[n])
        arrived(z_link.at[n], sem_zlr.at[n])
        return total_state * z_link[n] + z_state[n].astype(F32)

    reached = lax.fori_loop(0, z, z_turn, jnp.zeros((quarter, v_ref.shape[1]), F32))
    for n in range(RING):
        back_out[n] = reached
        reached = reached * x_link[n] + x_state[n]

    def back_copy(hop):
        to = (x + hop) % RING
        return pltpu.make_async_remote_copy(
            back_out.at[to],
            back_in.at[x],
            sem_bs.at[hop],
            sem_br.at[x],
            (z * RING + to, head),
            MESH,
        )

    for hop in (2, 1, 3):
        back_copy(hop).start()
    back_in[x] = back_out[x]
    for hop in range(1, RING):
        sender = (x + hop) % RING
        arrived(back_in.at[sender], sem_br.at[sender])

    carry = back_in[...].reshape(depth, v_ref.shape[1])
    lead_owner = jnp.where(ends[0:1, :] > 0.0, owner[0:1, :], -1.0)
    lead = (first_state[...] + jnp.exp(at_end[0:1, :]) * carry).astype(BF16)

    half, step_off = groups // 2, groups // 4
    relays = tuple((n, -1 if n % 2 == 0 else 1) for n in range(RING)) if step_off else ()
    order = order_of(groups)
    early = len(order) * 9 // 16

    def target(hop, turn):
        return ((z + hop + groups) % groups) * RING + (x + turn) % RING

    def finish(hop):
        def one(turn, none):
            n = target(hop, turn)
            slots[n] = jnp.where(
                jnp.broadcast_to(lead_owner == n.astype(F32), lead.shape), lead, slots[n]
            )
            return none

        lax.fori_loop(0, RING, one, 0)

    def direct(hop, turn):
        n = target(hop, turn)
        return pltpu.make_async_remote_copy(
            slots.at[n], incoming.at[place], sem_os.at[n], sem_or.at[place], (n, head), MESH
        )

    def first_leg(r):
        turn, way = relays[r]
        via = target(way * step_off, 0)
        return pltpu.make_async_remote_copy(
            slots.at[target(half, turn)],
            relay.at[r],
            sem_rs.at[r],
            sem_rr.at[r],
            (via, head),
            MESH,
        )

    def second_leg(r):
        turn, way = relays[r]
        source = target(-way * step_off, 0)
        return pltpu.make_async_remote_copy(
            relay.at[r],
            incoming.at[source],
            sem_fs.at[r],
            sem_or.at[source],
            (target(way * step_off, turn), head),
            MESH,
        )

    def fire(hop):
        if hop == half and relays:
            for r in range(len(relays)):
                first_leg(r).start()
            return

        def one(turn, none):
            direct(hop, turn).start()
            return none

        lax.fori_loop(1 if hop == 0 else 0, RING, one, 0)

    finish(order[0])
    pl.semaphore_wait(ready, groups - 1)
    for n, hop in enumerate(order):
        if n + 1 < len(order):
            finish(order[n + 1])
        if n < early:
            fire(hop)

    incoming[place] = slots[place]
    loads[4].wait()
    loads[6].wait()
    high = carry.astype(BF16)
    low = (carry - high.astype(F32)).astype(BF16)
    later = lax.broadcasted_iota(jnp.int32, (TILE, TILE), 0) - lax.broadcasted_iota(
        jnp.int32, (TILE, TILE), 1
    )

    def attend(t, none):
        rows = pl.ds(pl.multiple_of(t * TILE, TILE), TILE)
        queries = q_ref[rows, :]
        my_cum = cum_rows[pl.ds(t, 1), :]
        my_seg = seg_rows[pl.ds(t, 1), :]
        cum_col = spread_col(my_cum)
        seg_col = spread_col(my_seg)
        reach = spread_col(jnp.where(my_seg == 0.0, jnp.exp(my_cum), 0.0))
        brought = jnp.dot(queries, high, preferred_element_type=F32) + jnp.dot(
            queries, low, preferred_element_type=F32
        )

        def look(j, part):
            cols = pl.ds(pl.multiple_of(j * TILE, TILE), TILE)
            scores = jnp.dot(queries, raw_t[:, cols], preferred_element_type=F32)
            allowed = (seg_col == seg_rows[pl.ds(j, 1), :]) & (later + (t - j) * TILE >= 0)
            damping = jnp.exp(jnp.where(allowed, cum_col - cum_rows[pl.ds(j, 1), :], -jnp.inf))
            return part + jnp.dot(
                (scores * damping).astype(BF16), v_ref[cols, :], preferred_element_type=F32
            )

        out = lax.fori_loop(0, t + 1, look, brought * reach)
        mixed[rows, :] = out
        squares[pl.ds(t, 1), :] = jnp.sum(jnp.transpose(out * out), axis=0, keepdims=True)
        return none

    lax.fori_loop(0, tiles, attend, 0)

    for r in range(len(relays)):
        arrived(relay.at[r], sem_rr.at[r])
        second_leg(r).start()
    for hop in order[early:]:
        fire(hop)

    fold_rows = table_ref.shape[0]
    page_lane = lax.broadcasted_iota(jnp.int32, (owners, TILE), 1)
    wanted = lax.broadcasted_iota(jnp.int32, (owners, TILE), 0) + place * owners
    which = (page_lane // docs).astype(F32)

    def search(n, found):
        row = table_ref[pl.ds(n, 1), :]
        return jnp.where(row == wanted, which + (n * fold).astype(F32), found)

    found = lax.fori_loop(0, fold_rows, search, jnp.full((owners, TILE), -1.0, F32))
    found = jnp.max(found, axis=1, keepdims=True)
    eye = lax.broadcasted_iota(jnp.int32, (owners, owners), 0) == lax.broadcasted_iota(
        jnp.int32, (owners, owners), 1
    )
    source_ref[...] = jnp.sum(
        jnp.where(eye, jnp.broadcast_to(found, (owners, owners)), 0.0), axis=0, keepdims=True
    ).astype(jnp.int32)

    def square_copy(n):
        return pltpu.make_async_remote_copy(
            head_out.at[n],
            head_in.at[n],
            sem_hs.at[n],
            sem_hr.at[n],
            (place, partner(spans[n])),
            MESH,
        )

    energy = squares[...]
    for n in range(len(spans)):
        head_out[n] = energy
        square_copy(n).start()
        square_copy(n).wait_recv()
        energy = energy + head_in[n]
    cum_rows[...] = lax.rsqrt(energy / count + EPS)

    def normed(t, none):
        rows = pl.ds(pl.multiple_of(t * TILE, TILE), TILE)
        scale = spread_col(cum_rows[pl.ds(t, 1), :])
        attended_ref[rows, :] = (mixed[rows, :] * scale * gain_ref[...]).astype(BF16)
        return none

    lax.fori_loop(0, tiles, normed, 0)

    for hop in range(1, RING):
        for copy in x_copies(hop):
            copy.wait_send()
        back_copy(hop).wait_send()
    for hop in range(1, groups):

        @pl.when(z + hop < groups)
        def _():
            for copy in z_copies(hop):
                copy.wait_send()

    for n in range(len(spans)):
        square_copy(n).wait_send()
    for hop in order:
        if hop == half and relays:
            for r in range(len(relays)):
                first_leg(r).wait_send()
            continue

        def sent(turn, none):
            direct(hop, turn).wait_send()
            return none

        lax.fori_loop(1 if hop == 0 else 0, RING, sent, 0)

    def landed(n, none):
        sender = (place + n) % owners
        arrived(incoming.at[sender], sem_or.at[sender])
        return none

    lax.fori_loop(1, owners, landed, 0)
    for r in range(len(relays)):
        second_leg(r).wait_send()


def settle(source_ref, incoming_ref, attended_in, cache_ref, attended_ref, blank, sem, sem_two):
    rows = pltpu.make_async_copy(attended_in, attended_ref, sem_two)
    rows.start()
    blank[...] = jnp.zeros_like(blank)
    pages = cache_ref.shape[0]

    def begin(n, none):
        source = source_ref[0, n]

        @pl.when(source >= 0)
        def _():
            pltpu.make_async_copy(incoming_ref.at[source], cache_ref.at[n], sem).start()

        @pl.when(source < 0)
        def _():
            pltpu.make_async_copy(blank, cache_ref.at[n], sem).start()

        return none

    lax.fori_loop(0, pages, begin, 0, unroll=4)
    pltpu.make_async_copy(incoming_ref, cache_ref, sem).wait()
    rows.wait()


VMEM = pl.BlockSpec(memory_space=pltpu.VMEM)
SMEM = pl.BlockSpec(memory_space=pltpu.SMEM)
HBM = pl.BlockSpec(memory_space=pltpu.HBM)


def in_hbm(array):
    return pltpu.with_memory_space_constraint(array, pltpu.HBM)


def shards(query_rows, key_rows, value_rows, log_gate, norm_gain, doc_ends, doc_page):
    tokens, heads, depth = query_rows.shape
    width = value_rows.shape[2]
    devices, ranks = lax.axis_size("seq"), lax.axis_size("head")
    bounds = doc_ends.shape[0]
    groups = devices // RING
    quarter = depth // RING
    tiles = tokens // TILE
    table = doc_page.reshape(devices * bounds // TILE, TILE)
    dma = pltpu.SemaphoreType.DMA
    incoming, attended, source = pl.pallas_call(
        functools.partial(whole, groups, ranks, heads * ranks * width),
        out_shape=(
            jax.ShapeDtypeStruct((devices, depth, width), BF16),
            jax.ShapeDtypeStruct((tokens, width), BF16),
            jax.ShapeDtypeStruct((1, devices), jnp.int32),
        ),
        in_specs=[HBM] * 7,
        out_specs=(VMEM, VMEM, VMEM),
        scratch_shapes=[
            pltpu.VMEM((tokens, depth), BF16),
            pltpu.VMEM((tokens, depth), BF16),
            pltpu.VMEM((tokens, width), BF16),
            pltpu.VMEM((tiles, TILE), F32),
            pltpu.VMEM(table.shape, jnp.int32),
            pltpu.VMEM((1, bounds), jnp.int32),
            pltpu.VMEM((1, width), F32),
            pltpu.VMEM((devices, depth, width), BF16),
            pltpu.VMEM((RING, depth, width), BF16),
            pltpu.VMEM((tokens, width), F32),
            pltpu.VMEM((tiles, TILE), F32),
            pltpu.VMEM((tiles, TILE), F32),
            pltpu.VMEM((1, tokens), F32),
            pltpu.VMEM((tiles, TILE), F32),
            pltpu.VMEM((max(ranks.bit_length() - 1, 1), tiles, TILE), F32),
            pltpu.VMEM((max(ranks.bit_length() - 1, 1), tiles, TILE), F32),
            pltpu.VMEM((depth, tokens), BF16),
            pltpu.VMEM((depth, tokens), BF16),
            pltpu.VMEM((8 * depth, tokens), BF16),
            pltpu.VMEM((depth, width), F32),
            pltpu.VMEM((1, 1, TILE), F32),
            pltpu.VMEM((RING, quarter, width), F32),
            pltpu.VMEM((RING, 1, TILE), F32),
            pltpu.VMEM((quarter, width), BF16),
            pltpu.VMEM((1, 1, TILE), F32),
            pltpu.VMEM((groups, quarter, width), BF16),
            pltpu.VMEM((groups, 1, TILE), F32),
            pltpu.VMEM((RING, quarter, width), F32),
            pltpu.VMEM((RING, quarter, width), F32),
            pltpu.VMEM((depth, width), F32),
            pltpu.SemaphoreType.REGULAR,
            dma((7,)),
            dma((RING,)),
            dma((RING,)),
            dma((RING,)),
            dma((RING,)),
            dma((groups,)),
            dma((groups,)),
            dma((groups,)),
            dma((groups,)),
            dma((RING,)),
            dma((RING,)),
            dma((max(ranks.bit_length() - 1, 1),)),
            dma((max(ranks.bit_length() - 1, 1),)),
            dma((devices,)),
            dma((devices,)),
            dma((RING,)),
            dma((RING,)),
            dma((RING,)),
        ],
        compiler_params=pltpu.CompilerParams(
            collective_id=0, has_side_effects=True, vmem_limit_bytes=40 << 20
        ),
        name="whole",
    )(
        in_hbm(query_rows.reshape(tokens, depth)),
        in_hbm(key_rows.reshape(tokens, depth)),
        in_hbm(value_rows.reshape(tokens, width)),
        in_hbm(log_gate.reshape(tiles, TILE)),
        in_hbm(doc_ends.reshape(1, bounds)),
        in_hbm(table),
        in_hbm(norm_gain),
    )
    cache, attended = pl.pallas_call(
        settle,
        out_shape=(
            jax.ShapeDtypeStruct((devices, depth, width), BF16),
            jax.ShapeDtypeStruct((tokens, width), BF16),
        ),
        in_specs=[SMEM, VMEM, VMEM],
        out_specs=(HBM, HBM),
        scratch_shapes=[
            pltpu.VMEM((depth, width), BF16),
            pltpu.SemaphoreType.DMA,
            pltpu.SemaphoreType.DMA,
        ],
        compiler_params=pltpu.CompilerParams(vmem_limit_bytes=8 << 20),
        name="settle",
    )(source, incoming, attended)
    return attended.reshape(tokens, heads, width), cache.reshape(devices, heads, depth, width)


def solution(mesh):
    placed = (
        P("seq", "head", None),
        P("seq", "head", None),
        P("seq", "head", None),
        P("head", "seq"),
        P("head", None),
        P("seq"),
        P(),
    )
    return jax.shard_map(
        shards,
        mesh=mesh,
        in_specs=placed,
        out_specs=(P("seq", "head", None), P("seq", "head", None, None)),
        check_vma=False,
    )
```

```python
import functools

import jax
import jax.numpy as jnp
from jax import lax
from jax.experimental import pallas as pl
from jax.experimental.pallas import tpu as pltpu
from jax.sharding import PartitionSpec as P

EPS = 1e-05
RING = 4
TILE = 128
MESH = pl.DeviceIdType.MESH
F32 = jnp.float32
BF16 = jnp.bfloat16


def row_to_col(row):
    n = row.shape[1]
    eye = lax.broadcasted_iota(jnp.int32, (n, n), 0) == lax.broadcasted_iota(jnp.int32, (n, n), 1)
    return jnp.sum(jnp.where(eye, jnp.broadcast_to(row, (n, n)), 0.0), axis=1, keepdims=True)


def spread_col(row):
    n = row.shape[1]
    return jnp.transpose(jnp.broadcast_to(row, (n, n)))


def running_sum(gates):
    rows, lanes = gates.shape
    lane = lax.broadcasted_iota(jnp.int32, gates.shape, 1)
    sub = lax.broadcasted_iota(jnp.int32, gates.shape, 0)
    total = gates
    step = 1
    while step < lanes:
        total = total + jnp.where(lane >= step, pltpu.roll(total, step, 1), 0.0)
        step *= 2
    last = jnp.broadcast_to(total[:, lanes - 1 :], gates.shape)
    before = jnp.where(sub >= 1, pltpu.roll(last, 1, 0), 0.0)
    step = 1
    while step < rows:
        before = before + jnp.where(sub >= step, pltpu.roll(before, step, 0), 0.0)
        step *= 2
    return total + before


def order_of(groups):
    half = groups // 2
    order = [half]
    for hop in range(half - 1, 0, -1):
        order += [hop, -hop]
    return order + [0]


def whole(
    groups,
    heads,
    count,
    q_hbm,
    k_hbm,
    v_hbm,
    gate_hbm,
    ends_hbm,
    table_hbm,
    gain_hbm,
    incoming,
    attended_ref,
    source_ref,
    q_ref,
    k_ref,
    v_ref,
    gate_ref,
    table_ref,
    ends_ref,
    gain_ref,
    slots,
    relay,
    mixed,
    cum_rows,
    seg_rows,
    own_rows,
    squares,
    head_out,
    head_in,
    raw_t,
    scaled_t,
    lhs,
    state,
    link,
    x_state,
    x_link,
    z_out,
    z_link_out,
    z_state,
    z_link,
    back_out,
    back_in,
    first_state,
    lead_out,
    ready,
    sem_in,
    sem_xs,
    sem_xr,
    sem_xls,
    sem_xlr,
    sem_zs,
    sem_zr,
    sem_zls,
    sem_zlr,
    sem_bs,
    sem_br,
    sem_hs,
    sem_hr,
    sem_os,
    sem_or,
    sem_rs,
    sem_rr,
    sem_fs,
    sem_cs,
    sem_cr,
    sem_cf,
):
    place = lax.axis_index("seq")
    head = lax.axis_index("head")
    z, x = place // RING, place % RING
    tokens, depth = k_ref.shape
    tiles = tokens // TILE
    docs = ends_ref.shape[1]
    owners = slots.shape[0]
    quarter = depth // RING

    loads = [
        pltpu.make_async_copy(source, target, sem_in.at[n])
        for n, (source, target) in enumerate(
            (
                (gate_hbm, gate_ref),
                (table_hbm, table_ref),
                (k_hbm, k_ref),
                (v_hbm, v_ref),
                (q_hbm, q_ref),
                (ends_hbm, ends_ref),
                (gain_hbm, gain_ref),
            )
        )
    ]
    for load in loads:
        load.start()

    barrier = pltpu.get_barrier_semaphore()

    def target(hop, turn):
        return ((z + hop + groups) % groups) * RING + (x + turn) % RING

    spans = [1 << n for n in range((heads - 1).bit_length())]

    def partner(span):
        return head + span * (1 - 2 * ((head // span) % 2))

    def greet(semaphore, device):
        pl.semaphore_signal(semaphore, inc=1, device_id=device, device_id_type=MESH)

    reach_out = sorted(range(1, groups), key=lambda n: -min(n, groups - n))
    for hop in reach_out:
        greet(barrier, (((z + hop) % groups) * RING + x, head))
    for hop in (2, 1, 3):
        greet(barrier, (z * RING + (x + hop) % RING, head))
    for span in spans:
        greet(barrier, (place, partner(span)))
    ahead = max(1, 3 * groups // 16) if groups >= 4 else 0
    ways = (ahead, -ahead) if ahead else ()
    for way in ways:
        for turn in range(1, RING):
            greet(barrier, (target(way, turn), head))

    loads[0].wait()
    loads[1].wait()
    loads[5].wait()
    cum = running_sum(gate_ref[...])
    cum_rows[...] = cum
    ends = row_to_col(ends_ref[...].astype(F32))
    fold = TILE // docs
    pages = jnp.broadcast_to(table_ref[pl.ds(place // fold, 1), :], (8, TILE))
    aligned = pages
    for n in range(1, fold):
        here = jnp.full((8, TILE), place % fold, jnp.int32) == n
        aligned = jnp.where(here, pltpu.roll(pages, TILE - n * docs, 1), aligned)
    owner = row_to_col((aligned[0:1, :docs] >> (owners.bit_length() - 1)).astype(F32))
    used = ends > 0.0
    lane = lax.broadcasted_iota(jnp.int32, (docs, TILE), 1).astype(F32)
    doc = lax.broadcasted_iota(jnp.int32, (docs, TILE), 0).astype(F32)
    cum_row = [cum[t : t + 1, :] for t in range(tiles)]
    total = cum[tiles - 1 :, TILE - 1 :]
    seg_row = []
    at_end = jnp.zeros((docs, 1), F32)
    for t in range(tiles):
        position = lane + float(t * TILE)
        seg_row.append(
            jnp.sum(jnp.where(used & (ends <= position), 1.0, 0.0), axis=0, keepdims=True)
        )
        seg_rows[pl.ds(t, 1), :] = seg_row[t]
        at_end = at_end + jnp.sum(
            jnp.where(position == ends - 1.0, jnp.broadcast_to(cum_row[t], position.shape), 0.0),
            axis=1,
            keepdims=True,
        )
    loads[2].wait()
    loads[3].wait()
    for t in range(tiles):
        inside = (jnp.broadcast_to(seg_row[t], doc.shape) == doc) & used
        done = jnp.sum(jnp.where(inside, 1.0, 0.0), axis=0, keepdims=True)
        stop = jnp.sum(jnp.where(inside, at_end, 0.0), axis=0, keepdims=True)
        owned = jnp.sum(jnp.where(inside, owner, 0.0), axis=0, keepdims=True)
        stop = jnp.where(done > 0.0, stop, total)
        cols = pl.ds(t * TILE, TILE)
        own_rows[:, cols] = jnp.where(done > 0.0, owned, -1.0)
        keep = jnp.where(done > 0.0, 0.0, 1.0)
        weight = jnp.exp(stop - cum_row[t])
        turned = jnp.transpose(k_ref[cols, :].astype(F32))
        raw_t[:, cols] = turned.astype(BF16)
        turned = turned * weight
        high = turned.astype(BF16)
        scaled_t[:, cols] = high
        low = ((turned - high.astype(F32)) * keep).astype(BF16)
        values = v_ref[cols, :]
        piece = jnp.dot((high.astype(F32) * keep).astype(BF16), values, preferred_element_type=F32)
        piece = piece + jnp.dot(low, values, preferred_element_type=F32)
        if t == 0:
            state[...] = piece
        else:
            state[...] += piece
    any_ended = jnp.sum(jnp.where(used, 1.0, 0.0), axis=0, keepdims=True)
    through = jnp.where(any_ended > 0.0, 0.0, jnp.exp(total))
    link[0] = jnp.broadcast_to(through, (1, TILE))

    pl.semaphore_wait(barrier, groups + RING - 2 + len(spans) + len(ways) * (RING - 1))

    def x_copies(hop):
        to = (x + hop) % RING
        device = (z * RING + to, head)
        rows = pl.ds(pl.multiple_of(to * quarter, quarter), quarter)
        return (
            pltpu.make_async_remote_copy(
                state.at[rows], x_state.at[x], sem_xs.at[hop], sem_xr.at[x], device, MESH
            ),
            pltpu.make_async_remote_copy(
                link.at[0], x_link.at[x], sem_xls.at[hop], sem_xlr.at[x], device, MESH
            ),
        )

    def arrived(target, sem):
        pltpu.make_async_remote_copy(
            target, target, sem_in.at[0], sem, (place, head), MESH
        ).wait_recv()

    for hop in (2, 1, 3):
        for copy in x_copies(hop):
            copy.start()
    for hop in reach_out:
        greet(ready, (((z + hop) % groups) * RING + x, head))
    mine = pl.ds(pl.multiple_of(x * quarter, quarter), quarter)
    x_state[x] = state[mine, :]
    x_link[x] = link[0]
    def direct(hop, turn):
        n = target(hop, turn)
        return pltpu.make_async_remote_copy(
            slots.at[n], incoming.at[place], sem_os.at[n], sem_or.at[place], (n, head), MESH
        )

    def build(planes):
        for b, plane in enumerate(planes):
            for turn in range(RING):
                number = (plane * RING + turn).astype(F32)
                mask = jnp.where(own_rows[...] == number, 1.0, 0.0).astype(BF16)
                rows = pl.ds((b * RING + turn) * depth, depth)
                lhs[rows, :] = scaled_t[...] * mask
        count_rows = len(planes) * RING * depth
        result = jnp.dot(lhs[0:count_rows, :], v_ref[...], preferred_element_type=F32)
        result = result.astype(BF16).reshape(len(planes) * RING, depth, v_ref.shape[1])
        for b, plane in enumerate(planes):
            slots[pl.ds(plane * RING, RING)] = result[b * RING : (b + 1) * RING]

    if ways:
        build([(z + way + groups) % groups for way in ways])
    for hop in range(1, RING):
        sender = (x + hop) % RING
        arrived(x_state.at[sender], sem_xr.at[sender])
        arrived(x_link.at[sender], sem_xlr.at[sender])
    group_state, group_link = x_state[0], x_link[0]
    for n in range(1, RING):
        group_state = group_state * x_link[n] + x_state[n]
        group_link = group_link * x_link[n]
    z_out[...] = group_state.astype(BF16)
    z_link_out[0] = group_link

    def z_copies(hop):
        device = ((z + hop) * RING + x, head)
        return (
            pltpu.make_async_remote_copy(
                z_out, z_state.at[z], sem_zs.at[hop], sem_zr.at[z], device, MESH
            ),
            pltpu.make_async_remote_copy(
                z_link_out.at[0], z_link.at[z], sem_zls.at[hop], sem_zlr.at[z], device, MESH
            ),
        )

    for hop in reach_out:

        @pl.when(z + hop < groups)
        def _():
            for copy in z_copies(hop):
                copy.start()

    for turn in range(RING):
        for way in ways:
            direct(way, turn).start()

    own_all = own_rows[...]

    def remaining(n):
        if not ways:
            return n
        n = n + jnp.where(n >= ahead, 1, 0)
        n = n + jnp.where(n >= groups - ahead, 1, 0)
        return (z + n) % groups

    def slot_group(n, none):
        build([remaining(2 * n), remaining(2 * n + 1)])
        return none

    lax.fori_loop(0, (groups - len(ways)) // 2, slot_group, 0)
    leading = jnp.where((jnp.concatenate(seg_row, axis=1) == 0.0) & (own_all >= 0.0), 1.0, 0.0)
    first_state[...] = jnp.dot(
        scaled_t[...] * leading.astype(BF16), v_ref[...], preferred_element_type=F32
    )

    def z_turn(n, total_state):
        arrived(z_state.at[n], sem_zr.at[n])
        arrived(z_link.at[n], sem_zlr.at[n])
        return total_state * z_link[n] + z_state[n].astype(F32)

    reached = lax.fori_loop(0, z, z_turn, jnp.zeros((quarter, v_ref.shape[1]), F32))
    for n in range(RING):
        back_out[n] = reached
        reached = reached * x_link[n] + x_state[n]

    def back_copy(hop):
        to = (x + hop) % RING
        return pltpu.make_async_remote_copy(
            back_out.at[to],
            back_in.at[x],
            sem_bs.at[hop],
            sem_br.at[x],
            (z * RING + to, head),
            MESH,
        )

    for hop in (2, 1, 3):
        back_copy(hop).start()
    back_in[x] = back_out[x]
    for hop in range(1, RING):
        sender = (x + hop) % RING
        arrived(back_in.at[sender], sem_br.at[sender])

    carry = back_in[...].reshape(depth, v_ref.shape[1])
    lead_owner = jnp.where(ends[0:1, :] > 0.0, owner[0:1, :], -1.0)
    lead = (first_state[...] + jnp.exp(at_end[0:1, :]) * carry).astype(BF16)
    lead_out[...] = lead

    half, step_off = groups // 2, groups // 4
    relays = tuple((n, -1 if n % 2 == 0 else 1) for n in range(RING)) if step_off else ()
    order = [hop for hop in order_of(groups) if hop not in ways]
    early = (len(order) + 1) // 2

    def finish(hop):
        def one(turn, none):
            n = target(hop, turn)
            slots[n] = jnp.where(
                jnp.broadcast_to(lead_owner == n.astype(F32), lead.shape), lead, slots[n]
            )
            return none

        lax.fori_loop(0, RING, one, 0)

    def lead_copy(n):
        spot = owners + n * RING + x
        return pltpu.make_async_remote_copy(
            lead_out,
            incoming.at[spot],
            sem_cs.at[n],
            sem_cr.at[n * RING + x],
            (target(ways[n], 0), head),
            MESH,
        )

    def lead_spread(n, turn):
        spot = owners + n * RING + x
        return pltpu.make_async_remote_copy(
            incoming.at[spot],
            incoming.at[spot],
            sem_cf.at[n * RING + turn],
            sem_cr.at[n * RING + x],
            (target(0, turn), head),
            MESH,
        )

    def first_leg(r):
        turn, way = relays[r]
        via = target(way * step_off, 0)
        return pltpu.make_async_remote_copy(
            slots.at[target(half, turn)],
            relay.at[r],
            sem_rs.at[r],
            sem_rr.at[r],
            (via, head),
            MESH,
        )

    def second_leg(r):
        turn, way = relays[r]
        source = target(-way * step_off, 0)
        return pltpu.make_async_remote_copy(
            relay.at[r],
            incoming.at[source],
            sem_fs.at[r],
            sem_or.at[source],
            (target(way * step_off, turn), head),
            MESH,
        )

    def fire(hop):
        if hop == half and relays:
            for r in range(len(relays)):
                first_leg(r).start()
            return

        def one(turn, none):
            direct(hop, turn).start()
            return none

        lax.fori_loop(1 if hop == 0 else 0, RING, one, 0)

    finish(order[0])
    pl.semaphore_wait(ready, groups - 1)
    for n in range(len(ways)):
        lead_copy(n).start()
    for n, hop in enumerate(order):
        if n + 1 < len(order):
            finish(order[n + 1])
        if n < early:
            fire(hop)

    incoming[place] = slots[place]
    loads[4].wait()
    loads[6].wait()
    high = carry.astype(BF16)
    low = (carry - high.astype(F32)).astype(BF16)
    later = lax.broadcasted_iota(jnp.int32, (TILE, TILE), 0) - lax.broadcasted_iota(
        jnp.int32, (TILE, TILE), 1
    )

    def attend(t, none):
        rows = pl.ds(pl.multiple_of(t * TILE, TILE), TILE)
        queries = q_ref[rows, :]
        my_cum = cum_rows[pl.ds(t, 1), :]
        my_seg = seg_rows[pl.ds(t, 1), :]
        cum_col = spread_col(my_cum)
        seg_col = spread_col(my_seg)
        reach = spread_col(jnp.where(my_seg == 0.0, jnp.exp(my_cum), 0.0))
        brought = jnp.dot(queries, high, preferred_element_type=F32) + jnp.dot(
            queries, low, preferred_element_type=F32
        )

        def look(j, part):
            cols = pl.ds(pl.multiple_of(j * TILE, TILE), TILE)
            scores = jnp.dot(queries, raw_t[:, cols], preferred_element_type=F32)
            allowed = (seg_col == seg_rows[pl.ds(j, 1), :]) & (later + (t - j) * TILE >= 0)
            damping = jnp.exp(jnp.where(allowed, cum_col - cum_rows[pl.ds(j, 1), :], -jnp.inf))
            return part + jnp.dot(
                (scores * damping).astype(BF16), v_ref[cols, :], preferred_element_type=F32
            )

        out = lax.fori_loop(0, t + 1, look, brought * reach)
        mixed[rows, :] = out
        squares[pl.ds(t, 1), :] = jnp.sum(jnp.transpose(out * out), axis=0, keepdims=True)
        return none

    lax.fori_loop(0, tiles, attend, 0)

    for r in range(len(relays)):
        arrived(relay.at[r], sem_rr.at[r])
        second_leg(r).start()
    for n in range(len(ways)):
        arrived(incoming.at[owners + n * RING + x], sem_cr.at[n * RING + x])
        for turn in range(1, RING):
            lead_spread(n, turn).start()
    for hop in order[early:]:
        fire(hop)

    fold_rows = table_ref.shape[0]
    page_lane = lax.broadcasted_iota(jnp.int32, (owners, TILE), 1)
    wanted = lax.broadcasted_iota(jnp.int32, (owners, TILE), 0) + place * owners
    which = (page_lane // docs + jnp.where(page_lane % docs == 0, owners, 0)).astype(F32)

    def search(n, found):
        row = table_ref[pl.ds(n, 1), :]
        return jnp.where(row == wanted, which + (n * fold).astype(F32), found)

    found = lax.fori_loop(0, fold_rows, search, jnp.full((owners, TILE), -1.0, F32))
    found = jnp.max(found, axis=1, keepdims=True).astype(jnp.int32)
    leads_here = found >= owners
    sender_of = jnp.where(leads_here, found - owners, found)
    plane_of = sender_of >> (RING.bit_length() - 1)
    column_of = sender_of - plane_of * RING
    found = sender_of
    for n, way in enumerate(ways):
        match = leads_here & (plane_of == (z - way + groups) % groups)
        found = jnp.where(match, owners + n * RING + column_of, found)
    found = found.astype(F32)
    eye = lax.broadcasted_iota(jnp.int32, (owners, owners), 0) == lax.broadcasted_iota(
        jnp.int32, (owners, owners), 1
    )
    source_ref[...] = jnp.sum(
        jnp.where(eye, jnp.broadcast_to(found, (owners, owners)), 0.0), axis=0, keepdims=True
    ).astype(jnp.int32)

    def square_copy(n):
        return pltpu.make_async_remote_copy(
            head_out.at[n],
            head_in.at[n],
            sem_hs.at[n],
            sem_hr.at[n],
            (place, partner(spans[n])),
            MESH,
        )

    energy = squares[...]
    for n in range(len(spans)):
        head_out[n] = energy
        square_copy(n).start()
        square_copy(n).wait_recv()
        energy = energy + head_in[n]
    cum_rows[...] = lax.rsqrt(energy / count + EPS)

    def normed(t, none):
        rows = pl.ds(pl.multiple_of(t * TILE, TILE), TILE)
        scale = spread_col(cum_rows[pl.ds(t, 1), :])
        attended_ref[rows, :] = (mixed[rows, :] * scale * gain_ref[...]).astype(BF16)
        return none

    lax.fori_loop(0, tiles, normed, 0)

    for hop in range(1, RING):
        for copy in x_copies(hop):
            copy.wait_send()
        back_copy(hop).wait_send()
    for hop in range(1, groups):

        @pl.when(z + hop < groups)
        def _():
            for copy in z_copies(hop):
                copy.wait_send()

    for n in range(len(spans)):
        square_copy(n).wait_send()
    for hop in list(ways) + order:
        if hop == half and relays:
            for r in range(len(relays)):
                first_leg(r).wait_send()
            continue

        def sent(turn, none):
            direct(hop, turn).wait_send()
            return none

        lax.fori_loop(1 if hop == 0 else 0, RING, sent, 0)

    def landed(n, none):
        sender = (place + n) % owners
        arrived(incoming.at[sender], sem_or.at[sender])
        return none

    lax.fori_loop(1, owners, landed, 0)
    for r in range(len(relays)):
        second_leg(r).wait_send()
    for n in range(len(ways)):
        lead_copy(n).wait_send()
        for turn in range(1, RING):
            lead_spread(n, turn).wait_send()
            sender = (x + turn) % RING
            arrived(incoming.at[owners + n * RING + sender], sem_cr.at[n * RING + sender])


def settle(source_ref, incoming_ref, attended_in, cache_ref, attended_ref, blank, sem, sem_two):
    rows = pltpu.make_async_copy(attended_in, attended_ref, sem_two)
    rows.start()
    blank[...] = jnp.zeros_like(blank)
    pages = cache_ref.shape[0]

    def begin(n, none):
        source = source_ref[0, n]

        @pl.when(source >= 0)
        def _():
            pltpu.make_async_copy(incoming_ref.at[source], cache_ref.at[n], sem).start()

        @pl.when(source < 0)
        def _():
            pltpu.make_async_copy(blank, cache_ref.at[n], sem).start()

        return none

    lax.fori_loop(0, pages, begin, 0, unroll=4)
    pltpu.make_async_copy(incoming_ref.at[pl.ds(0, pages)], cache_ref, sem).wait()
    rows.wait()


VMEM = pl.BlockSpec(memory_space=pltpu.VMEM)
SMEM = pl.BlockSpec(memory_space=pltpu.SMEM)
HBM = pl.BlockSpec(memory_space=pltpu.HBM)


def in_hbm(array):
    return pltpu.with_memory_space_constraint(array, pltpu.HBM)


def shards(query_rows, key_rows, value_rows, log_gate, norm_gain, doc_ends, doc_page):
    tokens, heads, depth = query_rows.shape
    width = value_rows.shape[2]
    devices, ranks = lax.axis_size("seq"), lax.axis_size("head")
    bounds = doc_ends.shape[0]
    groups = devices // RING
    quarter = depth // RING
    tiles = tokens // TILE
    table = doc_page.reshape(devices * bounds // TILE, TILE)
    dma = pltpu.SemaphoreType.DMA
    incoming, attended, source = pl.pallas_call(
        functools.partial(whole, groups, ranks, heads * ranks * width),
        out_shape=(
            jax.ShapeDtypeStruct((devices + 2 * RING, depth, width), BF16),
            jax.ShapeDtypeStruct((tokens, width), BF16),
            jax.ShapeDtypeStruct((1, devices), jnp.int32),
        ),
        in_specs=[HBM] * 7,
        out_specs=(VMEM, VMEM, VMEM),
        scratch_shapes=[
            pltpu.VMEM((tokens, depth), BF16),
            pltpu.VMEM((tokens, depth), BF16),
            pltpu.VMEM((tokens, width), BF16),
            pltpu.VMEM((tiles, TILE), F32),
            pltpu.VMEM(table.shape, jnp.int32),
            pltpu.VMEM((1, bounds), jnp.int32),
            pltpu.VMEM((1, width), F32),
            pltpu.VMEM((devices, depth, width), BF16),
            pltpu.VMEM((RING, depth, width), BF16),
            pltpu.VMEM((tokens, width), F32),
            pltpu.VMEM((tiles, TILE), F32),
            pltpu.VMEM((tiles, TILE), F32),
            pltpu.VMEM((1, tokens), F32),
            pltpu.VMEM((tiles, TILE), F32),
            pltpu.VMEM((max(ranks.bit_length() - 1, 1), tiles, TILE), F32),
            pltpu.VMEM((max(ranks.bit_length() - 1, 1), tiles, TILE), F32),
            pltpu.VMEM((depth, tokens), BF16),
            pltpu.VMEM((depth, tokens), BF16),
            pltpu.VMEM((8 * depth, tokens), BF16),
            pltpu.VMEM((depth, width), F32),
            pltpu.VMEM((1, 1, TILE), F32),
            pltpu.VMEM((RING, quarter, width), F32),
            pltpu.VMEM((RING, 1, TILE), F32),
            pltpu.VMEM((quarter, width), BF16),
            pltpu.VMEM((1, 1, TILE), F32),
            pltpu.VMEM((groups, quarter, width), BF16),
            pltpu.VMEM((groups, 1, TILE), F32),
            pltpu.VMEM((RING, quarter, width), F32),
            pltpu.VMEM((RING, quarter, width), F32),
            pltpu.VMEM((depth, width), F32),
            pltpu.VMEM((depth, width), BF16),
            pltpu.SemaphoreType.REGULAR,
            dma((7,)),
            dma((RING,)),
            dma((RING,)),
            dma((RING,)),
            dma((RING,)),
            dma((groups,)),
            dma((groups,)),
            dma((groups,)),
            dma((groups,)),
            dma((RING,)),
            dma((RING,)),
            dma((max(ranks.bit_length() - 1, 1),)),
            dma((max(ranks.bit_length() - 1, 1),)),
            dma((devices,)),
            dma((devices,)),
            dma((RING,)),
            dma((RING,)),
            dma((RING,)),
            dma((2,)),
            dma((2 * RING,)),
            dma((2 * RING,)),
        ],
        compiler_params=pltpu.CompilerParams(
            collective_id=0, has_side_effects=True, vmem_limit_bytes=40 << 20
        ),
        name="whole",
    )(
        in_hbm(query_rows.reshape(tokens, depth)),
        in_hbm(key_rows.reshape(tokens, depth)),
        in_hbm(value_rows.reshape(tokens, width)),
        in_hbm(log_gate.reshape(tiles, TILE)),
        in_hbm(doc_ends.reshape(1, bounds)),
        in_hbm(table),
        in_hbm(norm_gain),
    )
    cache, attended = pl.pallas_call(
        settle,
        out_shape=(
            jax.ShapeDtypeStruct((devices, depth, width), BF16),
            jax.ShapeDtypeStruct((tokens, width), BF16),
        ),
        in_specs=[SMEM, VMEM, VMEM],
        out_specs=(HBM, HBM),
        scratch_shapes=[
            pltpu.VMEM((depth, width), BF16),
            pltpu.SemaphoreType.DMA,
            pltpu.SemaphoreType.DMA,
        ],
        compiler_params=pltpu.CompilerParams(vmem_limit_bytes=8 << 20),
        name="settle",
    )(source, incoming, attended)
    return attended.reshape(tokens, heads, width), cache.reshape(devices, heads, depth, width)


def solution(mesh):
    placed = (
        P("seq", "head", None),
        P("seq", "head", None),
        P("seq", "head", None),
        P("head", "seq"),
        P("head", None),
        P("seq"),
        P(),
    )
    return jax.shard_map(
        shards,
        mesh=mesh,
        in_specs=placed,
        out_specs=(P("seq", "head", None), P("seq", "head", None, None)),
        check_vma=False,
    )
```
